32 devices in a mesh: groups: 2 (over x), expo: 8 (over z, y), sky: 2 (over core).
Axes of the slice: x: 2, y: 2, z: 4, core: 2. Of those that a mesh axis runs over, the one named last changes fastest.
Arguments:
- exposures: bfloat16 [384, 256, 512], P(('groups', 'expo'), 'sky'), parts along dimension 0, may hold values from -8 to 8
- slot_ids: int32 [16, 24], P('groups'), parts along dimension 0, may hold values from 0 to 128, as said below
- row_range: int32 [256, 2], P('groups'), parts along dimension 0, may hold values from 1 to 256, as said below
- bad_bands: int32 [256, 4], P('groups'), parts along dimension 0, may hold values 0 or 1
- kernel_choice: int32 [256, 4], P('groups'), parts along dimension 0, may hold values from 0 to 9
- flux_scale: float32 [256], P('groups'), parts along dimension 0, may hold values from 0.25 to 4
- vert_taps: bfloat16 [20, 21], P('groups'), parts along dimension 0, may hold values from -0.6 to 1.6
- horiz_taps: bfloat16 [20, 21], P('groups'), parts along dimension 0, may hold values from -0.6 to 1.6
Outputs:
- coadd_plane: float32 [4, 128, 512], P(('groups', 'sky'), 'expo'), parts along dimension 0
- rejected_count: int32 [4, 128, 512], P(('groups', 'sky'), 'expo'), parts along dimension 0
The draws below stay inside these ranges and needn't reach their ends.
There are 2 independent parts, one for each index of `groups`. The reference program is written for one: setup_inputs(seed, part) draws one part's arguments, and reference() takes and returns one part's arrays. A program takes and returns all parts, laid end to end along the dimension named above; each array names one. Nothing has to cross between parts.
Inputs may be any that keep to these rules, and one draw needn't show every extreme that they name: `slot_ids`: each exposure number below 128 stands in exactly one slot; in each row the occupied slots come first and the others hold 128; a row has 8 to 24 occupied slots, and some row has all 24. `row_range`: column 0 is below 128 and column 1 is at least 128 and above column 0.
All inputs are finite; a program needn't handle non-finite values.
Results may differ from the reference program's by a relative error of at most 0.008.
Values may be sent and summed in bfloat16 or wider, within the bound.
A program may use at most 128 MiB of HBM per device.

```python
import math
import jax
import jax.numpy as jnp
from jax import lax

COLS = 512
BAND_COLS = 128
TAPS = 21
NKERN = 10
REJECT = 4
MIN_VALID = 12
EXP_MEAN = 16
ROW_DEV = 128
SLOTS = 24
EXPOSURES = 128
SLOTS_ALL = 192
NROWS = 256
BANDS = 4
N_EXPO = 8
N_SKY = 2


def draw_exposures(key, part):
    sky_field = jax.random.normal(jax.random.fold_in(key, 1), (NROWS, COLS), jnp.float32)
    jitter = jax.random.normal(jax.random.fold_in(key, 2), (SLOTS_ALL, NROWS, COLS), jnp.float32)
    return jnp.clip(sky_field[None] + jitter, -8.0, 8.0).astype(jnp.bfloat16)


def draw_slot_ids(key, part):
    pair_count = N_EXPO // 2
    half_mean = EXP_MEAN // 2
    imbalance = jax.random.randint(jax.random.fold_in(key, 11), (pair_count,), 0, half_mean + 1)
    imbalance = imbalance.at[0].set(half_mean)
    flipped = jax.random.randint(jax.random.fold_in(key, 12), (pair_count,), 0, 2)
    first_count = EXP_MEAN + imbalance * (1 - 2 * flipped)
    second_count = 2 * EXP_MEAN - first_count
    per_device = jnp.stack([first_count, second_count], 1).reshape(N_EXPO)
    shuffle = jax.random.permutation(jax.random.fold_in(key, 13), N_EXPO)
    per_device = per_device[shuffle]
    offsets = jnp.cumsum(per_device) - per_device
    numbers = jax.random.permutation(jax.random.fold_in(key, 14), EXPOSURES)
    slot_place = jnp.arange(SLOTS)
    position = jnp.clip(offsets[:, None] + slot_place[None, :], 0, EXPOSURES - 1)
    occupied = slot_place[None, :] < per_device[:, None]
    return jnp.where(occupied, numbers[position], EXPOSURES).astype(jnp.int32)


def draw_row_range(key, part):
    early_total = min(20, EXPOSURES // 2)
    strip_rows = NROWS // 8
    ranking = jax.random.permutation(jax.random.fold_in(key, 23), EXPOSURES)
    early = ranking < early_total
    early_first = jax.random.randint(jax.random.fold_in(key, 21), (EXPOSURES,), 1, strip_rows)
    later_first = jax.random.randint(jax.random.fold_in(key, 24), (EXPOSURES,), strip_rows, NROWS // 2)
    first_row = jnp.where(early, early_first, later_first)
    first_row = jnp.where(ranking == 0, 1, first_row)
    extent = jax.random.randint(jax.random.fold_in(key, 22), (EXPOSURES,), NROWS // 2, NROWS + 1)
    last_row = jnp.minimum(first_row + extent, NROWS)
    last_row = jnp.where(ranking == 0, NROWS, last_row)
    return jnp.stack([first_row, last_row], 1).astype(jnp.int32)


def filter_bank(key):
    spread = jnp.clip(0.2 * jax.random.normal(key, (NKERN, TAPS), jnp.float32), -0.55, 0.55)
    centre = (jnp.arange(TAPS) == TAPS // 2).astype(jnp.float32)
    return (spread + centre[None, :]).astype(jnp.bfloat16)


def draw_vert_taps(key, part):
    return filter_bank(jax.random.fold_in(key, 31))


def draw_horiz_taps(key, part):
    return filter_bank(jax.random.fold_in(key, 32))


def plant(drawn, key, least, high):
    spot = [jax.random.randint(jax.random.fold_in(key, axis), (), 0, length) for axis, length in enumerate(drawn.shape)]
    longest = drawn.shape.index(max(drawn.shape))
    beside = spot[:longest] + [(spot[longest] + 1) % drawn.shape[longest]] + spot[longest + 1:]
    return drawn.at[tuple(spot)].set(least).at[tuple(beside)].set(high)


def setup_inputs(seed: int = 0, part: int = 0) -> dict:
    splits = jax.random.split(jax.random.key(seed), 9)
    part_keys = jax.random.split(jax.random.fold_in(splits[8], part), 9)
    return {
        "exposures": draw_exposures(jax.random.fold_in(jax.random.fold_in(splits[8], part), 71), part),
        "slot_ids": draw_slot_ids(jax.random.fold_in(jax.random.fold_in(splits[8], part), 71), part),
        "row_range": draw_row_range(jax.random.fold_in(jax.random.fold_in(splits[8], part), 71), part),
        "bad_bands": plant((jax.random.randint(part_keys[3], (EXPOSURES, BANDS), 0, 8) < 1).astype(jnp.int32), jax.random.fold_in(part_keys[3], 1), 0, 1),
        "kernel_choice": plant(jax.random.randint(part_keys[4], (EXPOSURES, BANDS), 0, NKERN), jax.random.fold_in(part_keys[4], 1), 0, NKERN - 1).astype(jnp.int32),
        "flux_scale": jnp.clip(jnp.exp(jax.random.uniform(part_keys[5], (EXPOSURES,), jnp.float32, math.log(0.25), math.log(4.0))), 0.25, 4.0),
        "vert_taps": draw_vert_taps(jax.random.fold_in(jax.random.fold_in(splits[8], part), 71), part),
        "horiz_taps": draw_horiz_taps(jax.random.fold_in(jax.random.fold_in(splits[8], part), 71), part),
    }


SENTINEL = 1.0e30


def filter_slot(picture, vertical_taps, horizontal_taps):
    margin = TAPS // 2
    band_index = jnp.arange(COLS, dtype=jnp.int32) // BAND_COLS
    column_vertical = vertical_taps[band_index]
    column_horizontal = horizontal_taps[band_index]
    padded = jnp.pad(picture.astype(jnp.float32), ((margin, margin), (0, 0)))
    vertical = jnp.zeros((NROWS, COLS), jnp.float32)
    for offset in range(TAPS):
        vertical = vertical + column_vertical[:, offset][None, :] * padded[offset:offset + NROWS, :]
    rounded = lax.optimization_barrier(vertical.astype(jnp.bfloat16)).astype(jnp.float32)
    widened = jnp.pad(rounded, ((0, 0), (margin, margin)))
    horizontal = jnp.zeros((NROWS, COLS), jnp.float32)
    for offset in range(TAPS):
        horizontal = horizontal + column_horizontal[:, offset][None, :] * widened[:, offset:offset + COLS]
    return horizontal


def one_slot(packed):
    picture, vertical_taps, horizontal_taps, factor = packed
    return (filter_slot(picture, vertical_taps, horizontal_taps) * factor).astype(jnp.bfloat16)


def in_groups(tensor):
    return tensor.reshape((SLOTS_ALL // 8, 8) + tensor.shape[1:])


def reference(exposures, slot_ids, row_range, bad_bands, kernel_choice, flux_scale, vert_taps, horiz_taps):
    slot_list = slot_ids.reshape(-1)
    occupied = slot_list < EXPOSURES
    lookup = jnp.minimum(slot_list, EXPOSURES - 1)
    chosen = kernel_choice[lookup]
    slot_vertical = vert_taps.astype(jnp.float32)[chosen]
    slot_horizontal = horiz_taps.astype(jnp.float32)[chosen]
    slot_scale = flux_scale[lookup]
    planes = lax.map(jax.vmap(one_slot), (in_groups(exposures), in_groups(slot_vertical), in_groups(slot_horizontal), in_groups(slot_scale)))
    planes = planes.reshape(SLOTS_ALL, NROWS, COLS)
    row_index = jnp.arange(NROWS, dtype=jnp.int32)
    row_usable = (row_index[None, :] >= row_range[lookup, 0][:, None]) & (row_index[None, :] < row_range[lookup, 1][:, None]) & occupied[:, None]
    band_index = jnp.arange(COLS, dtype=jnp.int32) // BAND_COLS
    column_usable = (bad_bands[lookup] == 0)[:, band_index]

    def one_row(row_number):
        values = lax.dynamic_index_in_dim(planes, row_number, 1, keepdims=False).astype(jnp.float32)
        usable = lax.dynamic_index_in_dim(row_usable, row_number, 1, keepdims=False)[:, None] & column_usable
        cover_count = jnp.sum(usable.astype(jnp.int32), axis=0, dtype=jnp.int32)
        grand_total = jnp.sum(jnp.where(usable, values, 0.0), axis=0)
        highest = lax.top_k(jnp.where(usable, values, -SENTINEL).T, REJECT)[0]
        lowest = lax.top_k(jnp.where(usable, -values, -SENTINEL).T, REJECT)[0]
        top_sum = jnp.sum(highest, axis=1)
        bottom_sum = -jnp.sum(lowest, axis=1)
        clipped = cover_count >= MIN_VALID
        used_count = jnp.where(clipped, cover_count - 2 * REJECT, cover_count)
        kept_sum = jnp.where(clipped, grand_total - top_sum - bottom_sum, grand_total)
        coadd_rows = kept_sum / jnp.maximum(used_count, 1).astype(jnp.float32)
        return coadd_rows, (EXPOSURES - used_count).astype(jnp.int32)

    coadd_plane, rejected_count = lax.map(one_row, row_index)
    return coadd_plane.reshape(N_SKY, ROW_DEV, COLS), rejected_count.reshape(N_SKY, ROW_DEV, COLS)
```

```python
import functools

import jax
import jax.numpy as jnp
from jax import lax
from jax.experimental import pallas as pl
from jax.experimental.pallas import tpu as pltpu
from jax.sharding import PartitionSpec as P

BAND_COLS = 128
TAPS = 21
REJECT = 4
MIN_VALID = 12


SENTINEL = 1e30
HIGHEST = lax.Precision.HIGHEST


def padded_2(cells, sides, width):
    for axis, dim in sides:
        count = lax.axis_size(axis)
        ends = count - 1
        head = lax.slice_in_dim(cells, 0, width, axis=dim)
        tail = lax.slice_in_dim(cells, cells.shape[dim] - width, cells.shape[dim], axis=dim)
        cells = jnp.concatenate(
            [
                lax.ppermute(tail, axis, [(i, (i + 1) % count) for i in range(ends)]),
                cells,
                lax.ppermute(head, axis, [((i + 1) % count, i) for i in range(ends)]),
            ],
            axis=dim,
        )
    return cells


def shift_table(outputs, taps):
    out_index = jnp.arange(outputs, dtype=jnp.int32)[None, :, None]
    in_index = jnp.arange(outputs + taps - 1, dtype=jnp.int32)[None, None, :]
    offsets = jnp.arange(taps, dtype=jnp.int32)[:, None, None]
    return (in_index - out_index == offsets).astype(jnp.bfloat16)


def compare_pair(entries, first_place, second_place):
    larger = jnp.maximum(entries[first_place], entries[second_place])
    smaller = jnp.minimum(entries[first_place], entries[second_place])
    entries[first_place] = larger
    entries[second_place] = smaller


def leading_four(values):
    grouped = values.reshape((values.shape[0] // 4, 4) + values.shape[1:])
    entries = [grouped[:, position] for position in range(4)]
    for first_place, second_place in ((0, 1), (2, 3), (0, 2), (1, 3), (1, 2)):
        compare_pair(entries, first_place, second_place)
    while entries[0].shape[0] > 1:
        if entries[0].shape[0] % 2:
            entries = [
                jnp.concatenate(
                    [member, jnp.full((1,) + member.shape[1:], -SENTINEL, member.dtype)], 0
                )
                for member in entries
            ]
        middle = entries[0].shape[0] // 2
        merged = [
            jnp.maximum(entries[position][:middle], entries[3 - position][middle:])
            for position in range(4)
        ]
        for first_place, second_place in ((0, 2), (1, 3), (0, 1), (2, 3)):
            compare_pair(merged, first_place, second_place)
        entries = merged
    return jnp.concatenate(entries, 0)


def usable_mask(slot_list, first_row, row_count, row_range, bad_bands, exposures_total):
    lookup = jnp.minimum(slot_list, exposures_total - 1)
    picker = (lookup[:, None] == jnp.arange(exposures_total, dtype=jnp.int32)[None, :]).astype(
        jnp.float32
    )
    bounds = jnp.dot(picker, row_range.astype(jnp.float32), precision=HIGHEST)
    flagged = jnp.dot(picker, bad_bands.astype(jnp.float32), precision=HIGHEST)
    row_place = (first_row + jnp.arange(row_count, dtype=jnp.int32)).astype(jnp.float32)
    row_fine = (
        (row_place[None, :] >= bounds[:, 0:1])
        & (row_place[None, :] < bounds[:, 1:2])
        & (slot_list < exposures_total)[:, None]
    )
    column_fine = jnp.repeat(flagged < 0.5, BAND_COLS, axis=1)
    return row_fine[:, :, None] & column_fine[:, None, :]


def usable_count(first_row, row_count, row_range, bad_bands):
    row_place = (first_row + jnp.arange(row_count, dtype=jnp.int32)).astype(jnp.float32)
    bounds = row_range.astype(jnp.float32)
    covered = (
        (row_place[None, :] >= bounds[:, 0:1]) & (row_place[None, :] < bounds[:, 1:2])
    ).astype(jnp.float32)
    clean = (bad_bands == 0).astype(jnp.float32)
    per_band = jnp.dot(covered.T, clean, precision=HIGHEST)
    return jnp.repeat(per_band, BAND_COLS, axis=1).astype(jnp.int32)


def finish_pixels(grand_total, top_sum, bottom_sum, cover_count, exposures_total):
    clipped = cover_count >= MIN_VALID
    used_count = jnp.where(clipped, cover_count - 2 * REJECT, cover_count)
    kept_sum = jnp.where(clipped, grand_total - top_sum - bottom_sum, grand_total)
    coadd_plane = kept_sum / jnp.maximum(used_count, 1).astype(jnp.float32)
    return (coadd_plane, exposures_total - used_count)


def general_shards(
    exposures, slot_ids, row_range, bad_bands, kernel_choice, flux_scale, vert_taps, horiz_taps
):
    slot_count, row_dev, columns = exposures.shape
    exposures_total = flux_scale.shape[0]
    kernels = vert_taps.shape[0]
    margin = TAPS // 2
    band_count = columns // BAND_COLS
    expo_size = lax.axis_size("expo")
    expo_place = lax.axis_index("expo")
    sky_place = lax.axis_index("sky")
    negative_fill = jnp.asarray(-SENTINEL, jnp.bfloat16)
    own_slots = lax.dynamic_index_in_dim(slot_ids, expo_place, 0, keepdims=False)
    own_lookup = jnp.minimum(own_slots, exposures_total - 1)
    picker = (own_lookup[:, None] == jnp.arange(exposures_total, dtype=jnp.int32)[None, :]).astype(
        jnp.float32
    )
    chosen = jnp.dot(picker, kernel_choice.astype(jnp.float32), precision=HIGHEST)
    selector = (chosen[:, :, None] == jnp.arange(kernels, dtype=jnp.float32)[None, None, :]).astype(
        jnp.bfloat16
    )
    factor = jnp.dot(picker, flux_scale, precision=HIGHEST)
    block_rows = min(row_dev, 128)
    vertical_bank = jnp.einsum(
        "kt,tij->kij", vert_taps, shift_table(block_rows, TAPS), preferred_element_type=jnp.float32
    ).astype(jnp.bfloat16)
    vertical_pick = jnp.einsum(
        "sbk,kij->sbij", selector, vertical_bank, preferred_element_type=jnp.float32
    ).astype(jnp.bfloat16)
    widened = padded_2(exposures, (("sky", 1),), margin)
    widened = widened.reshape(slot_count, row_dev + 2 * margin, band_count, BAND_COLS)
    vertical_blocks = jnp.einsum(
        "sbij,sjbc->sibc", vertical_pick, widened, preferred_element_type=jnp.float32
    )
    vertical = vertical_blocks.astype(jnp.bfloat16).reshape(slot_count, row_dev, columns)
    horizontal_bank = jnp.einsum(
        "kt,tcj->kjc", horiz_taps, shift_table(BAND_COLS, TAPS), preferred_element_type=jnp.float32
    ).astype(jnp.bfloat16)
    horizontal_pick = jnp.einsum(
        "sbk,kjc->sbjc", selector, horizontal_bank, preferred_element_type=jnp.float32
    ).astype(jnp.bfloat16)
    padded = jnp.pad(vertical, ((0, 0), (0, 0), (margin, margin)))
    strips = jnp.stack(
        [
            padded[:, :, band_number * BAND_COLS : band_number * BAND_COLS + BAND_COLS + 2 * margin]
            for band_number in range(band_count)
        ],
        2,
    )
    filtered = jnp.einsum(
        "srbj,sbjc->srbc", strips, horizontal_pick, preferred_element_type=jnp.float32
    )
    planes = (filtered.reshape(slot_count, row_dev, columns) * factor[:, None, None]).astype(
        jnp.bfloat16
    )
    rows_out = row_dev // expo_size
    first_row = sky_place * row_dev + expo_place * rows_out
    cover_count = usable_count(first_row, rows_out, row_range, bad_bands)
    own_usable = usable_mask(
        own_slots, sky_place * row_dev, row_dev, row_range, bad_bands, exposures_total
    )
    partial_total = jnp.sum(
        jnp.where(own_usable, planes, jnp.zeros((), jnp.bfloat16)), axis=0, dtype=jnp.float32
    )[None]
    own_high = leading_four(jnp.where(own_usable, planes, negative_fill).reshape(slot_count, -1))
    own_low = leading_four(jnp.where(own_usable, -planes, negative_fill).reshape(slot_count, -1))
    extremes = jnp.concatenate([own_high, own_low], 0).reshape(8, row_dev, columns)
    received = lax.all_to_all(partial_total, "expo", split_axis=1, concat_axis=0, tiled=True)
    grand_total = jnp.sum(received, axis=0)
    arrived = lax.all_to_all(extremes, "expo", split_axis=1, concat_axis=0, tiled=True)
    senders = arrived.shape[0] // 8
    out_rows = arrived.shape[1]
    out_cols = arrived.shape[2]
    grouped = arrived.reshape(senders, 8, out_rows * out_cols)
    best_high = leading_four(grouped[:, :4].reshape(senders * 4, out_rows * out_cols))
    best_low = leading_four(grouped[:, 4:].reshape(senders * 4, out_rows * out_cols))
    high_sum = jnp.sum(best_high.astype(jnp.float32), axis=0).reshape(out_rows, out_cols)
    low_sum = -jnp.sum(best_low.astype(jnp.float32), axis=0).reshape(out_rows, out_cols)
    coadd_plane, rejected_count = finish_pixels(
        grand_total, high_sum, low_sum, cover_count, exposures_total
    )
    return (coadd_plane[None], rejected_count[None])


LANES = 128
FILL = 2.0**100
HALO = 16
SORT_FOUR = ((0, 1), (2, 3), (0, 2), (1, 3), (1, 2))
SORT_BITONIC = ((0, 2), (1, 3), (0, 1), (2, 3))


def exchange(entries, places, first, second):
    for a, b in places:
        entries[a], entries[b] = first(entries[a], entries[b]), second(entries[a], entries[b])
    return entries


def merge_four(left, right, first, second, ordered=True):
    merged = [first(left[i], right[3 - i]) for i in range(4)]
    if ordered:
        exchange(merged, SORT_BITONIC, first, second)
    return merged


def flip_bit(place, bit):
    weight = 1 << bit
    return place + weight * (1 - 2 * ((place // weight) % 2))


def flip_mask(place, mask, steps):
    for bit in range(steps):
        if mask >> bit & 1:
            place = flip_bit(place, bit)
    return place


def low_bit(mask, steps):
    for bit in range(steps):
        if mask >> bit & 1:
            return bit
    return steps


def fused_kernel(
    senders,
    slot_ids,
    row_range,
    bad_bands,
    kernel_choice,
    flux_scale,
    taps,
    range_table,
    band_table,
    exposures,
    coadd,
    rejected,
    pixels,
    vertical_bank,
    horizontal_bank,
    planes,
    extremes,
    totals,
    got_extremes,
    got_totals,
    load_sem,
    halo_send,
    halo_recv,
    ext_send,
    ext_recv,
    tot_send,
    tot_recv,
):
    slots, row_dev, columns = exposures.shape
    exposures_total = flux_scale.shape[0]
    kernels = vertical_bank.shape[0]
    bands = columns // BAND_COLS
    margin = TAPS // 2
    rows_out = row_dev // senders
    steps = senders.bit_length() - 1
    place = lax.axis_index("expo")
    sky = lax.axis_index("sky")

    for slot in range(slots):
        pltpu.make_async_copy(
            exposures.at[slot], pixels.at[slot, pl.ds(0, row_dev)], load_sem.at[slot]
        ).start()

    barrier = pltpu.get_barrier_semaphore()
    pl.semaphore_signal(barrier, 1, device_id={"sky": 1 - sky})
    for bit in range(steps):
        pl.semaphore_signal(barrier, 1, device_id={"expo": flip_bit(place, bit)})
    pl.semaphore_wait(barrier, steps + 1)

    edge = pl.multiple_of((1 - sky) * (row_dev - HALO), HALO)
    halo = pltpu.make_async_remote_copy(
        src_ref=exposures.at[:, pl.ds(edge, HALO)],
        dst_ref=pixels.at[:, pl.ds(row_dev, HALO)],
        send_sem=halo_send,
        recv_sem=halo_recv,
        device_id={"sky": 1 - sky},
    )
    halo.start()

    near = (
        jnp.abs(
            lax.broadcasted_iota(jnp.int32, (LANES, LANES), 0)
            - lax.broadcasted_iota(jnp.int32, (LANES, LANES), 1)
        )
        <= margin
    )

    @pl.loop(0, kernels)
    def _(k):
        def circulant(row):
            spread = jnp.broadcast_to(taps[pl.ds(row, 1), :], (LANES, LANES))
            return pltpu.roll(spread, LANES - margin + margin % 8, 1, stride=1, stride_axis=0)

        vertical = circulant(k)
        outer = jnp.where(near, 0.0, vertical)
        outer = jnp.where(sky == 0, outer, pltpu.roll(outer, HALO, 1))
        vertical_bank[k, :, 0:LANES] = jnp.where(near, vertical, 0.0).astype(jnp.bfloat16)
        vertical_bank[k, :, LANES : LANES + HALO] = outer[:, :HALO].astype(jnp.bfloat16)
        horizontal = circulant(kernels + k)
        horizontal_bank[k, 0:LANES, :] = jnp.where(near, horizontal, 0.0).astype(jnp.bfloat16)
        horizontal_bank[k, LANES : 2 * LANES, :] = jnp.where(near, 0.0, horizontal).astype(
            jnp.bfloat16
        )

    row_place = lax.broadcasted_iota(jnp.int32, (row_dev, LANES), 0) + sky * row_dev
    from_right = lax.broadcasted_iota(jnp.int32, (row_dev, LANES), 1) < LANES // 2

    halo.wait_recv()

    @pl.loop(0, slots)
    def _(slot):
        pltpu.make_async_copy(
            exposures.at[slot], pixels.at[slot, pl.ds(0, row_dev)], load_sem.at[slot]
        ).wait()
        number = slot_ids[place, slot]
        entry = jnp.minimum(number, exposures_total - 1)
        factor = flux_scale[entry]
        first_row = row_range[entry, 0]
        end_row = jnp.where(number < exposures_total, row_range[entry, 1], 0)
        chosen = [kernel_choice[entry, band] for band in range(bands)]
        vertical = [
            jnp.dot(
                vertical_bank[chosen[band]],
                pixels[slot, :, band * LANES : (band + 1) * LANES],
                preferred_element_type=jnp.float32,
            )
            for band in range(bands)
        ]
        none = jnp.zeros((row_dev, LANES), jnp.float32)
        for band in range(bands):
            right = vertical[band + 1] if band + 1 < bands else none
            left = vertical[band - 1] if band else none
            strip = jnp.concatenate(
                [vertical[band], jnp.where(from_right, right, left)], axis=1
            ).astype(jnp.bfloat16)
            filtered = jnp.dot(
                strip, horizontal_bank[chosen[band]], preferred_element_type=jnp.float32
            )
            last_row = jnp.where(bad_bands[entry, band] == 0, end_row, 0)
            usable = (row_place >= first_row) & (row_place < last_row)
            shown = jnp.where(usable, filtered * factor, -FILL).astype(jnp.bfloat16)
            planes[slot, :, :, band * LANES : (band + 1) * LANES] = shown.reshape(
                senders, rows_out, LANES
            )

    def reduce_block(block):
        @pl.loop(0, bands)
        def _(band):
            cols = pl.ds(pl.multiple_of(band * LANES, LANES), LANES)
            empty = jnp.asarray(-FILL, jnp.bfloat16)
            high = low = None
            total = jnp.zeros((rows_out, LANES), jnp.float32)
            for group in range(slots // 4):
                upper = [planes[4 * group + i, block, :, cols] for i in range(4)]
                lower = []
                for i in range(4):
                    gone = upper[i] == empty
                    lower.append(jnp.where(gone, -empty, upper[i]))
                    total += jnp.where(gone, jnp.zeros((), jnp.bfloat16), upper[i]).astype(
                        jnp.float32
                    )
                exchange(upper, SORT_FOUR, jnp.maximum, jnp.minimum)
                exchange(lower, SORT_FOUR, jnp.minimum, jnp.maximum)
                high = merge_four(high, upper, jnp.maximum, jnp.minimum) if group else upper
                low = merge_four(low, lower, jnp.minimum, jnp.maximum) if group else lower
            for i in range(4):
                extremes[block, i, :, cols] = high[i]
                extremes[block, 4 + i, :, cols] = low[i]
            totals[block, :, cols] = total

    slot_of = {}
    for bit in range(steps):
        for mask in range(0, senders, 2 << bit):
            slot_of[bit, mask] = len(slot_of)

    def copies(mask):
        bit = low_bit(mask, steps)
        block = flip_mask(place, mask, steps)
        landing = slot_of[bit, mask ^ (1 << bit)]
        target = {"expo": flip_bit(place, bit)}
        return (
            pltpu.make_async_remote_copy(
                src_ref=extremes.at[block],
                dst_ref=got_extremes.at[landing],
                send_sem=ext_send.at[landing],
                recv_sem=ext_recv.at[landing],
                device_id=target,
            ),
            pltpu.make_async_remote_copy(
                src_ref=totals.at[block],
                dst_ref=got_totals.at[landing],
                send_sem=tot_send.at[landing],
                recv_sem=tot_recv.at[landing],
                device_id=target,
            ),
        )

    started = []

    def send(mask):
        for copy in copies(mask):
            copy.start()
            started.append(copy)

    def arrive(bit, mask):
        for copy in copies(mask ^ (1 << bit)):
            copy.wait_recv()
        return slot_of[bit, mask]

    for mask in range(senders - 1, 0, -2):
        reduce_block(flip_mask(place, mask, steps))
        send(mask)
    for mask in range(senders - 2, -1, -2):
        reduce_block(flip_mask(place, mask, steps))

    for mask in range(senders - 2, 0, -2):
        block = flip_mask(place, mask, steps)
        for bit in range(low_bit(mask, steps)):
            landing = arrive(bit, mask)

            @pl.loop(0, bands)
            def _(band):
                cols = pl.ds(pl.multiple_of(band * LANES, LANES), LANES)
                mine = [extremes[block, i, :, cols] for i in range(8)]
                theirs = [got_extremes[landing, i, :, cols] for i in range(8)]
                high = merge_four(mine[:4], theirs[:4], jnp.maximum, jnp.minimum)
                low = merge_four(mine[4:], theirs[4:], jnp.minimum, jnp.maximum)
                for i in range(4):
                    extremes[block, i, :, cols] = high[i]
                    extremes[block, 4 + i, :, cols] = low[i]
                totals[block, :, cols] += got_totals[landing, :, cols]

        send(mask)

    first_out = sky * row_dev + place * rows_out
    out_place = lax.broadcasted_iota(jnp.int32, (exposures_total, LANES), 1) + first_out
    covered = (out_place >= range_table[:, 0:1]) & (out_place < range_table[:, 1:2])
    covered = jnp.where(covered, 1.0, 0.0)
    clean = jnp.concatenate(
        [
            jnp.broadcast_to(
                jnp.where(band_table[:, band : band + 1] == 0, 1.0, 0.0), (exposures_total, LANES)
            )
            for band in range(bands)
        ],
        axis=1,
    )
    counts = lax.dot_general(
        covered.astype(jnp.bfloat16),
        clean.astype(jnp.bfloat16),
        (((0,), (0,)), ((), ())),
        preferred_element_type=jnp.float32,
    )[:rows_out]

    landings = [arrive(bit, 0) for bit in range(steps)]
    for band in range(bands):
        cols = slice(band * LANES, (band + 1) * LANES)
        high = [extremes[place, i, :, cols] for i in range(4)]
        low = [extremes[place, 4 + i, :, cols] for i in range(4)]
        total = totals[place, :, cols]
        for landing in landings:
            ordered = landing != landings[-1]
            high = merge_four(
                high,
                [got_extremes[landing, i, :, cols] for i in range(4)],
                jnp.maximum,
                jnp.minimum,
                ordered,
            )
            low = merge_four(
                low,
                [got_extremes[landing, 4 + i, :, cols] for i in range(4)],
                jnp.minimum,
                jnp.maximum,
                ordered,
            )
            total += got_totals[landing, :, cols]
        outer = sum(entry.astype(jnp.float32) for entry in high) + sum(
            entry.astype(jnp.float32) for entry in low
        )
        count = counts[:, cols]
        clipped = count >= MIN_VALID
        used = jnp.where(clipped, count - 2 * REJECT, count)
        kept = jnp.where(clipped, total - outer, total)
        coadd[0, :, cols] = kept / jnp.maximum(used, 1.0)
        rejected[0, :, cols] = (exposures_total - used).astype(jnp.int32)

    halo.wait_send()
    for copy in started:
        copy.wait_send()


def fused_shards(
    exposures, slot_ids, row_range, bad_bands, kernel_choice, flux_scale, vert_taps, horiz_taps
):
    slots, row_dev, columns = exposures.shape
    senders = lax.axis_size("expo")
    kernels = vert_taps.shape[0]
    rows_out = row_dev // senders
    taps = jnp.concatenate([vert_taps, horiz_taps[:, ::-1]], 0).astype(jnp.float32)
    ahead = TAPS // 2 % 8
    blank = jnp.zeros((2 * kernels, LANES - TAPS), jnp.float32)
    taps = jnp.concatenate([taps[:, ahead:], blank, taps[:, :ahead]], 1)
    smem = pl.BlockSpec(memory_space=pltpu.SMEM)
    vmem = pl.BlockSpec(memory_space=pltpu.VMEM)
    landings = senders - 1
    return pl.pallas_call(
        functools.partial(fused_kernel, senders),
        out_shape=(
            jax.ShapeDtypeStruct((1, rows_out, columns), jnp.float32),
            jax.ShapeDtypeStruct((1, rows_out, columns), jnp.int32),
        ),
        in_specs=[smem] * 5 + [vmem] * 3 + [pl.BlockSpec(memory_space=pl.ANY)],
        out_specs=(vmem, vmem),
        scratch_shapes=[
            pltpu.VMEM((slots, row_dev + HALO, columns), jnp.bfloat16),
            pltpu.VMEM((kernels, LANES, LANES + HALO), jnp.bfloat16),
            pltpu.VMEM((kernels, 2 * LANES, LANES), jnp.bfloat16),
            pltpu.VMEM((slots, senders, rows_out, columns), jnp.bfloat16),
            pltpu.VMEM((senders, 8, rows_out, columns), jnp.bfloat16),
            pltpu.VMEM((senders, rows_out, columns), jnp.float32),
            pltpu.VMEM((landings, 8, rows_out, columns), jnp.bfloat16),
            pltpu.VMEM((landings, rows_out, columns), jnp.float32),
            pltpu.SemaphoreType.DMA((slots,)),
            pltpu.SemaphoreType.DMA,
            pltpu.SemaphoreType.DMA,
            pltpu.SemaphoreType.DMA((landings,)),
            pltpu.SemaphoreType.DMA((landings,)),
            pltpu.SemaphoreType.DMA((landings,)),
            pltpu.SemaphoreType.DMA((landings,)),
        ],
        compiler_params=pltpu.CompilerParams(collective_id=0, has_side_effects=True),
    )(
        slot_ids,
        row_range,
        bad_bands,
        kernel_choice,
        flux_scale,
        taps,
        row_range,
        bad_bands,
        exposures,
    )


def shards(
    exposures, slot_ids, row_range, bad_bands, kernel_choice, flux_scale, vert_taps, horiz_taps
):
    slots, row_dev, columns = exposures.shape
    senders = lax.axis_size("expo")
    fits = (
        lax.axis_size("sky") == 2
        and senders & (senders - 1) == 0
        and senders > 1
        and row_dev == LANES
        and row_dev % (senders * 16) == 0
        and slots % 4 == 0
        and columns % LANES == 0
    )
    chosen = fused_shards if fits else general_shards
    return chosen(
        exposures, slot_ids, row_range, bad_bands, kernel_choice, flux_scale, vert_taps, horiz_taps
    )


def solution(mesh):
    in_specs = (
        P(("groups", "expo"), "sky", None),
        P("groups", None),
        P("groups", None),
        P("groups", None),
        P("groups", None),
        P("groups"),
        P("groups", None),
        P("groups", None),
    )
    out_specs = (P(("groups", "sky"), "expo", None), P(("groups", "sky"), "expo", None))
    return jax.shard_map(shards, mesh=mesh, in_specs=in_specs, out_specs=out_specs, check_vma=False)
```

```python
import functools

import jax
import jax.numpy as jnp
from jax import lax
from jax.experimental import pallas as pl
from jax.experimental.pallas import tpu as pltpu
from jax.sharding import PartitionSpec as P

BAND_COLS = 128
TAPS = 21
REJECT = 4
MIN_VALID = 12


SENTINEL = 1e30
HIGHEST = lax.Precision.HIGHEST


def padded_2(cells, sides, width):
    for axis, dim in sides:
        count = lax.axis_size(axis)
        ends = count - 1
        head = lax.slice_in_dim(cells, 0, width, axis=dim)
        tail = lax.slice_in_dim(cells, cells.shape[dim] - width, cells.shape[dim], axis=dim)
        cells = jnp.concatenate(
            [
                lax.ppermute(tail, axis, [(i, (i + 1) % count) for i in range(ends)]),
                cells,
                lax.ppermute(head, axis, [((i + 1) % count, i) for i in range(ends)]),
            ],
            axis=dim,
        )
    return cells


def shift_table(outputs, taps):
    out_index = jnp.arange(outputs, dtype=jnp.int32)[None, :, None]
    in_index = jnp.arange(outputs + taps - 1, dtype=jnp.int32)[None, None, :]
    offsets = jnp.arange(taps, dtype=jnp.int32)[:, None, None]
    return (in_index - out_index == offsets).astype(jnp.bfloat16)


def compare_pair(entries, first_place, second_place):
    larger = jnp.maximum(entries[first_place], entries[second_place])
    smaller = jnp.minimum(entries[first_place], entries[second_place])
    entries[first_place] = larger
    entries[second_place] = smaller


def leading_four(values):
    grouped = values.reshape((values.shape[0] // 4, 4) + values.shape[1:])
    entries = [grouped[:, position] for position in range(4)]
    for first_place, second_place in ((0, 1), (2, 3), (0, 2), (1, 3), (1, 2)):
        compare_pair(entries, first_place, second_place)
    while entries[0].shape[0] > 1:
        if entries[0].shape[0] % 2:
            entries = [
                jnp.concatenate(
                    [member, jnp.full((1,) + member.shape[1:], -SENTINEL, member.dtype)], 0
                )
                for member in entries
            ]
        middle = entries[0].shape[0] // 2
        merged = [
            jnp.maximum(entries[position][:middle], entries[3 - position][middle:])
            for position in range(4)
        ]
        for first_place, second_place in ((0, 2), (1, 3), (0, 1), (2, 3)):
            compare_pair(merged, first_place, second_place)
        entries = merged
    return jnp.concatenate(entries, 0)


def usable_mask(slot_list, first_row, row_count, row_range, bad_bands, exposures_total):
    lookup = jnp.minimum(slot_list, exposures_total - 1)
    picker = (lookup[:, None] == jnp.arange(exposures_total, dtype=jnp.int32)[None, :]).astype(
        jnp.float32
    )
    bounds = jnp.dot(picker, row_range.astype(jnp.float32), precision=HIGHEST)
    flagged = jnp.dot(picker, bad_bands.astype(jnp.float32), precision=HIGHEST)
    row_place = (first_row + jnp.arange(row_count, dtype=jnp.int32)).astype(jnp.float32)
    row_fine = (
        (row_place[None, :] >= bounds[:, 0:1])
        & (row_place[None, :] < bounds[:, 1:2])
        & (slot_list < exposures_total)[:, None]
    )
    column_fine = jnp.repeat(flagged < 0.5, BAND_COLS, axis=1)
    return row_fine[:, :, None] & column_fine[:, None, :]


def usable_count(first_row, row_count, row_range, bad_bands):
    row_place = (first_row + jnp.arange(row_count, dtype=jnp.int32)).astype(jnp.float32)
    bounds = row_range.astype(jnp.float32)
    covered = (
        (row_place[None, :] >= bounds[:, 0:1]) & (row_place[None, :] < bounds[:, 1:2])
    ).astype(jnp.float32)
    clean = (bad_bands == 0).astype(jnp.float32)
    per_band = jnp.dot(covered.T, clean, precision=HIGHEST)
    return jnp.repeat(per_band, BAND_COLS, axis=1).astype(jnp.int32)


def finish_pixels(grand_total, top_sum, bottom_sum, cover_count, exposures_total):
    clipped = cover_count >= MIN_VALID
    used_count = jnp.where(clipped, cover_count - 2 * REJECT, cover_count)
    kept_sum = jnp.where(clipped, grand_total - top_sum - bottom_sum, grand_total)
    coadd_plane = kept_sum / jnp.maximum(used_count, 1).astype(jnp.float32)
    return (coadd_plane, exposures_total - used_count)


def general_shards(
    exposures, slot_ids, row_range, bad_bands, kernel_choice, flux_scale, vert_taps, horiz_taps
):
    slot_count, row_dev, columns = exposures.shape
    exposures_total = flux_scale.shape[0]
    kernels = vert_taps.shape[0]
    margin = TAPS // 2
    band_count = columns // BAND_COLS
    expo_size = lax.axis_size("expo")
    expo_place = lax.axis_index("expo")
    sky_place = lax.axis_index("sky")
    negative_fill = jnp.asarray(-SENTINEL, jnp.bfloat16)
    own_slots = lax.dynamic_index_in_dim(slot_ids, expo_place, 0, keepdims=False)
    own_lookup = jnp.minimum(own_slots, exposures_total - 1)
    picker = (own_lookup[:, None] == jnp.arange(exposures_total, dtype=jnp.int32)[None, :]).astype(
        jnp.float32
    )
    chosen = jnp.dot(picker, kernel_choice.astype(jnp.float32), precision=HIGHEST)
    selector = (chosen[:, :, None] == jnp.arange(kernels, dtype=jnp.float32)[None, None, :]).astype(
        jnp.bfloat16
    )
    factor = jnp.dot(picker, flux_scale, precision=HIGHEST)
    block_rows = min(row_dev, 128)
    vertical_bank = jnp.einsum(
        "kt,tij->kij", vert_taps, shift_table(block_rows, TAPS), preferred_element_type=jnp.float32
    ).astype(jnp.bfloat16)
    vertical_pick = jnp.einsum(
        "sbk,kij->sbij", selector, vertical_bank, preferred_element_type=jnp.float32
    ).astype(jnp.bfloat16)
    widened = padded_2(exposures, (("sky", 1),), margin)
    widened = widened.reshape(slot_count, row_dev + 2 * margin, band_count, BAND_COLS)
    vertical_blocks = jnp.einsum(
        "sbij,sjbc->sibc", vertical_pick, widened, preferred_element_type=jnp.float32
    )
    vertical = vertical_blocks.astype(jnp.bfloat16).reshape(slot_count, row_dev, columns)
    horizontal_bank = jnp.einsum(
        "kt,tcj->kjc", horiz_taps, shift_table(BAND_COLS, TAPS), preferred_element_type=jnp.float32
    ).astype(jnp.bfloat16)
    horizontal_pick = jnp.einsum(
        "sbk,kjc->sbjc", selector, horizontal_bank, preferred_element_type=jnp.float32
    ).astype(jnp.bfloat16)
    padded = jnp.pad(vertical, ((0, 0), (0, 0), (margin, margin)))
    strips = jnp.stack(
        [
            padded[:, :, band_number * BAND_COLS : band_number * BAND_COLS + BAND_COLS + 2 * margin]
            for band_number in range(band_count)
        ],
        2,
    )
    filtered = jnp.einsum(
        "srbj,sbjc->srbc", strips, horizontal_pick, preferred_element_type=jnp.float32
    )
    planes = (filtered.reshape(slot_count, row_dev, columns) * factor[:, None, None]).astype(
        jnp.bfloat16
    )
    rows_out = row_dev // expo_size
    first_row = sky_place * row_dev + expo_place * rows_out
    cover_count = usable_count(first_row, rows_out, row_range, bad_bands)
    own_usable = usable_mask(
        own_slots, sky_place * row_dev, row_dev, row_range, bad_bands, exposures_total
    )
    partial_total = jnp.sum(
        jnp.where(own_usable, planes, jnp.zeros((), jnp.bfloat16)), axis=0, dtype=jnp.float32
    )[None]
    own_high = leading_four(jnp.where(own_usable, planes, negative_fill).reshape(slot_count, -1))
    own_low = leading_four(jnp.where(own_usable, -planes, negative_fill).reshape(slot_count, -1))
    extremes = jnp.concatenate([own_high, own_low], 0).reshape(8, row_dev, columns)
    received = lax.all_to_all(partial_total, "expo", split_axis=1, concat_axis=0, tiled=True)
    grand_total = jnp.sum(received, axis=0)
    arrived = lax.all_to_all(extremes, "expo", split_axis=1, concat_axis=0, tiled=True)
    senders = arrived.shape[0] // 8
    out_rows = arrived.shape[1]
    out_cols = arrived.shape[2]
    grouped = arrived.reshape(senders, 8, out_rows * out_cols)
    best_high = leading_four(grouped[:, :4].reshape(senders * 4, out_rows * out_cols))
    best_low = leading_four(grouped[:, 4:].reshape(senders * 4, out_rows * out_cols))
    high_sum = jnp.sum(best_high.astype(jnp.float32), axis=0).reshape(out_rows, out_cols)
    low_sum = -jnp.sum(best_low.astype(jnp.float32), axis=0).reshape(out_rows, out_cols)
    coadd_plane, rejected_count = finish_pixels(
        grand_total, high_sum, low_sum, cover_count, exposures_total
    )
    return (coadd_plane[None], rejected_count[None])


LANES = 128
FILL = 2.0**100
HALO = 16
UNROLL = 4
SORT_FOUR = ((0, 1), (2, 3), (0, 2), (1, 3), (1, 2))
SORT_BITONIC = ((0, 2), (1, 3), (0, 1), (2, 3))


def exchange(entries, places, first, second):
    for a, b in places:
        entries[a], entries[b] = first(entries[a], entries[b]), second(entries[a], entries[b])
    return entries


def merge_four(left, right, first, second, ordered=True):
    merged = [first(left[i], right[3 - i]) for i in range(4)]
    if ordered:
        exchange(merged, SORT_BITONIC, first, second)
    return merged


def flip_bit(place, bit):
    weight = 1 << bit
    return place + weight * (1 - 2 * ((place // weight) % 2))


def bit_order(band, steps):
    order = list(range(steps))
    if steps > 1 and band % 4 == 1:
        order[0], order[1] = order[1], order[0]
    return order


def flip_mask(place, mask, order):
    for position, bit in enumerate(order):
        if mask >> position & 1:
            place = flip_bit(place, bit)
    return place


def low_bit(mask, steps):
    for position in range(steps):
        if mask >> position & 1:
            return position
    return steps


def multiples(level, steps):
    masks = range(0, 1 << steps, 1 << level)
    return sorted(masks, key=lambda mask: -int(format(mask, f"0{steps}b")[::-1], 2))


def fused_kernel(
    senders,
    slot_ids,
    row_range,
    bad_bands,
    kernel_choice,
    flux_scale,
    range_table,
    band_table,
    vert_taps,
    horiz_taps,
    exposures,
    kept_out,
    used_out,
    pixels,
    taps,
    vertical_bank,
    horizontal_bank,
    columns_done,
    planes,
    extremes,
    totals,
    got_extremes,
    got_totals,
    load_sem,
    halo_send,
    halo_recv,
    ext_send,
    ext_recv,
    tot_send,
    tot_recv,
):
    slots, row_dev, columns = exposures.shape
    exposures_total = flux_scale.shape[0]
    kernels = vertical_bank.shape[0]
    bands = columns // BAND_COLS
    margin = TAPS // 2
    rows_out = row_dev // senders
    steps = senders.bit_length() - 1
    place = lax.axis_index("expo")
    sky = lax.axis_index("sky")

    for slot in range(slots):
        pltpu.make_async_copy(
            exposures.at[slot], pixels.at[slot, pl.ds(0, row_dev)], load_sem.at[slot]
        ).start()

    barrier = pltpu.get_barrier_semaphore()
    pl.semaphore_signal(barrier, 1, device_id={"sky": 1 - sky})
    for bit in range(steps):
        pl.semaphore_signal(barrier, 1, device_id={"expo": flip_bit(place, bit)})
    pl.semaphore_wait(barrier, steps + 1)

    edge = pl.multiple_of((1 - sky) * (row_dev - HALO), HALO)
    halo = pltpu.make_async_remote_copy(
        src_ref=exposures.at[:, pl.ds(edge, HALO)],
        dst_ref=pixels.at[:, pl.ds(row_dev, HALO)],
        send_sem=halo_send,
        recv_sem=halo_recv,
        device_id={"sky": 1 - sky},
    )
    halo.start()

    near = (
        jnp.abs(
            lax.broadcasted_iota(jnp.int32, (LANES, LANES), 0)
            - lax.broadcasted_iota(jnp.int32, (LANES, LANES), 1)
        )
        <= margin
    )

    taps[...] = jnp.zeros_like(taps)
    taps[0, 0:kernels, 0:TAPS] = vert_taps[...].astype(jnp.float32)
    taps[1, 0:kernels, 0:TAPS] = horiz_taps[...].astype(jnp.float32)
    for side in range(2):
        taps[side] = pltpu.roll(taps[side], LANES - margin % 8, 1)

    @pl.loop(0, kernels)
    def _(k):
        def circulant(side):
            spread = jnp.broadcast_to(taps[side, pl.ds(k, 1), :], (LANES, LANES))
            return pltpu.roll(spread, LANES - margin + margin % 8, 1, stride=1, stride_axis=0)

        vertical = circulant(0)
        outer = jnp.where(near, 0.0, vertical)
        outer = jnp.where(sky == 0, outer, pltpu.roll(outer, HALO, 1))
        vertical_bank[k, :, 0:LANES] = jnp.where(near, vertical, 0.0).astype(jnp.bfloat16)
        vertical_bank[k, :, LANES : LANES + HALO] = outer[:, :HALO].astype(jnp.bfloat16)
        horizontal = circulant(1).T
        horizontal_bank[k, 0:LANES, :] = jnp.where(near, horizontal, 0.0).astype(jnp.bfloat16)
        horizontal_bank[k, LANES : 2 * LANES, :] = jnp.where(near, 0.0, horizontal).astype(
            jnp.bfloat16
        )

    row_place = lax.broadcasted_iota(jnp.int32, (row_dev, LANES), 0) + sky * row_dev
    from_right = lax.broadcasted_iota(jnp.int32, (row_dev, LANES), 1) < LANES // 2

    halo.wait_recv()
    for slot in range(slots):
        pltpu.make_async_copy(
            exposures.at[slot], pixels.at[slot, pl.ds(0, row_dev)], load_sem.at[slot]
        ).wait()

    def entry_of(slot):
        return jnp.minimum(slot_ids[place, slot], exposures_total - 1)

    def filter_rows(slot, band):
        done = jnp.dot(
            vertical_bank[kernel_choice[band, entry_of(slot)]],
            pixels[slot, :, band * LANES : (band + 1) * LANES],
            preferred_element_type=jnp.float32,
        ).astype(jnp.bfloat16)
        columns_done[band, slot] = done
        return done

    def filter_band(band):
        @pl.loop(0, slots // UNROLL)
        def _(group):
            members = [group * UNROLL + i for i in range(UNROLL)]
            if band == 0:
                middle = [filter_rows(slot, 0) for slot in members]
            else:
                middle = [columns_done[band, slot] for slot in members]
            if band + 1 < bands:
                right = [filter_rows(slot, band + 1) for slot in members]
            for i, slot in enumerate(members):
                side = jnp.zeros((row_dev, LANES), jnp.float32)
                left = columns_done[band - 1, slot].astype(jnp.float32) if band else side
                side = right[i].astype(jnp.float32) if band + 1 < bands else side
                outer = jnp.where(from_right, side, left).astype(jnp.bfloat16)
                number = slot_ids[place, slot]
                entry = entry_of(slot)
                filtered = jnp.dot(
                    jnp.concatenate([middle[i], outer], axis=1),
                    horizontal_bank[kernel_choice[band, entry]],
                    preferred_element_type=jnp.float32,
                )
                open_band = (number < exposures_total) & (bad_bands[band, entry] == 0)
                last_row = jnp.where(open_band, row_range[1, entry], 0)
                usable = (row_place >= row_range[0, entry]) & (row_place < last_row)
                shown = jnp.where(usable, filtered * flux_scale[entry], -FILL)
                planes[slot] = shown.astype(jnp.bfloat16).reshape(senders, rows_out, LANES)

    def reduce_block(band, block):
        empty = jnp.asarray(-FILL, jnp.bfloat16)
        high = low = None
        total = jnp.zeros((rows_out, LANES), jnp.float32)
        for group in range(slots // 4):
            upper = [planes[4 * group + i, block] for i in range(4)]
            lower = []
            for i in range(4):
                gone = upper[i] == empty
                lower.append(jnp.where(gone, -empty, upper[i]))
                total += jnp.where(gone, jnp.zeros((), jnp.bfloat16), upper[i]).astype(jnp.float32)
            exchange(upper, SORT_FOUR, jnp.maximum, jnp.minimum)
            exchange(lower, SORT_FOUR, jnp.minimum, jnp.maximum)
            high = merge_four(high, upper, jnp.maximum, jnp.minimum) if group else upper
            low = merge_four(low, lower, jnp.minimum, jnp.maximum) if group else lower
        for i in range(4):
            extremes[band, block, i] = high[i]
            extremes[band, block, 4 + i] = low[i]
        totals[band, block] = total

    slot_of = {}
    for bit in range(steps):
        for mask in range(0, senders, 2 << bit):
            slot_of[bit, mask] = len(slot_of)

    def copies(band, mask):
        order = bit_order(band, steps)
        level = low_bit(mask, steps)
        block = flip_mask(place, mask, order)
        landing = slot_of[level, mask ^ (1 << level)]
        target = {"expo": flip_bit(place, order[level])}
        return (
            pltpu.make_async_remote_copy(
                src_ref=extremes.at[band, block],
                dst_ref=got_extremes.at[band, landing],
                send_sem=ext_send.at[band, landing],
                recv_sem=ext_recv.at[band, landing],
                device_id=target,
            ),
            pltpu.make_async_remote_copy(
                src_ref=totals.at[band, block],
                dst_ref=got_totals.at[band, landing],
                send_sem=tot_send.at[band, landing],
                recv_sem=tot_recv.at[band, landing],
                device_id=target,
            ),
        )

    started = []

    def send(band, mask):
        for copy in copies(band, mask):
            copy.start()
            started.append(copy)

    def start_band(band):
        filter_band(band)
        for mask in multiples(0, steps):
            reduce_block(band, flip_mask(place, mask, bit_order(band, steps)))
            if mask % 2:
                send(band, mask)

    def forward(band, level):
        for mask in multiples(level, steps):
            for copy in copies(band, mask ^ (1 << (level - 1))):
                copy.wait_recv()
            landing = slot_of[level - 1, mask]
            block = flip_mask(place, mask, bit_order(band, steps))
            mine = [extremes[band, block, i] for i in range(8)]
            theirs = [got_extremes[band, landing, i] for i in range(8)]
            ordered = level < steps
            high = merge_four(mine[:4], theirs[:4], jnp.maximum, jnp.minimum, ordered)
            low = merge_four(mine[4:], theirs[4:], jnp.minimum, jnp.maximum, ordered)
            total = totals[band, block] + got_totals[band, landing]
            if level == steps:
                finish(band, high, low, total)
                continue
            for i in range(4):
                extremes[band, block, i] = high[i]
                extremes[band, block, 4 + i] = low[i]
            totals[band, block] = total
            if low_bit(mask, steps) == level:
                send(band, mask)

    first_out = sky * row_dev + place * rows_out

    def finish(band, high, low, total):
        cols = slice(band * LANES, (band + 1) * LANES)
        out_place = lax.broadcasted_iota(jnp.int32, (rows_out, exposures_total), 0) + first_out
        covered = (out_place >= range_table[0:1, :]) & (out_place < range_table[1:2, :])
        clean = jnp.where(band_table[band : band + 1, :] == 0, 1.0, 0.0)
        count = lax.dot_general(
            jnp.where(covered, 1.0, 0.0).astype(jnp.bfloat16),
            jnp.broadcast_to(clean, (LANES, exposures_total)).astype(jnp.bfloat16),
            (((1,), (1,)), ((), ())),
            preferred_element_type=jnp.float32,
        )
        outer = sum(entry.astype(jnp.float32) for entry in high) + sum(
            entry.astype(jnp.float32) for entry in low
        )
        clipped = count >= MIN_VALID
        kept_out[0, :, cols] = jnp.where(clipped, total - outer, total)
        used_out[0, :, cols] = jnp.where(clipped, count - 2 * REJECT, count)

    for turn in range(bands + steps):
        if turn < bands:
            start_band(turn)
        for level in range(1, steps + 1):
            if 0 <= turn - level < bands:
                forward(turn - level, level)

    halo.wait_send()
    for copy in started:
        copy.wait_send()


def fused_shards(
    exposures, slot_ids, row_range, bad_bands, kernel_choice, flux_scale, vert_taps, horiz_taps
):
    slots, row_dev, columns = exposures.shape
    senders = lax.axis_size("expo")
    kernels = vert_taps.shape[0]
    rows_out = row_dev // senders
    smem = pl.BlockSpec(memory_space=pltpu.SMEM)
    vmem = pl.BlockSpec(memory_space=pltpu.VMEM)
    landings = senders - 1
    bands = columns // LANES
    kept, used = pl.pallas_call(
        functools.partial(fused_kernel, senders),
        out_shape=(
            jax.ShapeDtypeStruct((1, rows_out, columns), jnp.float32),
            jax.ShapeDtypeStruct((1, rows_out, columns), jnp.float32),
        ),
        in_specs=[smem] * 5 + [vmem] * 4 + [pl.BlockSpec(memory_space=pl.ANY)],
        out_specs=(vmem, vmem),
        scratch_shapes=[
            pltpu.VMEM((slots, row_dev + HALO, columns), jnp.bfloat16),
            pltpu.VMEM((2, -(-kernels // 8) * 8, LANES), jnp.float32),
            pltpu.VMEM((kernels, LANES, LANES + HALO), jnp.bfloat16),
            pltpu.VMEM((kernels, 2 * LANES, LANES), jnp.bfloat16),
            pltpu.VMEM((bands, slots, row_dev, LANES), jnp.bfloat16),
            pltpu.VMEM((slots, senders, rows_out, LANES), jnp.bfloat16),
            pltpu.VMEM((bands, senders, 8, rows_out, LANES), jnp.bfloat16),
            pltpu.VMEM((bands, senders, rows_out, LANES), jnp.float32),
            pltpu.VMEM((bands, landings, 8, rows_out, LANES), jnp.bfloat16),
            pltpu.VMEM((bands, landings, rows_out, LANES), jnp.float32),
            pltpu.SemaphoreType.DMA((slots,)),
            pltpu.SemaphoreType.DMA,
            pltpu.SemaphoreType.DMA,
            pltpu.SemaphoreType.DMA((bands, landings)),
            pltpu.SemaphoreType.DMA((bands, landings)),
            pltpu.SemaphoreType.DMA((bands, landings)),
            pltpu.SemaphoreType.DMA((bands, landings)),
        ],
        compiler_params=pltpu.CompilerParams(collective_id=0, has_side_effects=True),
    )(
        slot_ids,
        row_range.T,
        bad_bands.T,
        kernel_choice.T,
        flux_scale,
        row_range.T,
        bad_bands.T,
        vert_taps,
        horiz_taps,
        exposures,
    )
    rejected = flux_scale.shape[0] - used.astype(jnp.int32)
    return kept / jnp.maximum(used, 1.0), rejected


def shards(
    exposures, slot_ids, row_range, bad_bands, kernel_choice, flux_scale, vert_taps, horiz_taps
):
    slots, row_dev, columns = exposures.shape
    senders = lax.axis_size("expo")
    fits = (
        lax.axis_size("sky") == 2
        and senders & (senders - 1) == 0
        and senders > 1
        and row_dev == LANES
        and row_dev % (senders * 16) == 0
        and slots % max(4, UNROLL) == 0
        and columns % LANES == 0
    )
    chosen = fused_shards if fits else general_shards
    return chosen(
        exposures, slot_ids, row_range, bad_bands, kernel_choice, flux_scale, vert_taps, horiz_taps
    )


def solution(mesh):
    in_specs = (
        P(("groups", "expo"), "sky", None),
        P("groups", None),
        P("groups", None),
        P("groups", None),
        P("groups", None),
        P("groups"),
        P("groups", None),
        P("groups", None),
    )
    out_specs = (P(("groups", "sky"), "expo", None), P(("groups", "sky"), "expo", None))
    return jax.shard_map(shards, mesh=mesh, in_specs=in_specs, out_specs=out_specs, check_vma=False)
```

```python
import functools

import jax
import jax.numpy as jnp
from jax import lax
from jax.experimental import pallas as pl
from jax.experimental.pallas import tpu as pltpu
from jax.sharding import PartitionSpec as P

BAND_COLS = 128
TAPS = 21
REJECT = 4
MIN_VALID = 12


SENTINEL = 1e30
HIGHEST = lax.Precision.HIGHEST


def padded_2(cells, sides, width):
    for axis, dim in sides:
        count = lax.axis_size(axis)
        ends = count - 1
        head = lax.slice_in_dim(cells, 0, width, axis=dim)
        tail = lax.slice_in_dim(cells, cells.shape[dim] - width, cells.shape[dim], axis=dim)
        cells = jnp.concatenate(
            [
                lax.ppermute(tail, axis, [(i, (i + 1) % count) for i in range(ends)]),
                cells,
                lax.ppermute(head, axis, [((i + 1) % count, i) for i in range(ends)]),
            ],
            axis=dim,
        )
    return cells


def shift_table(outputs, taps):
    out_index = jnp.arange(outputs, dtype=jnp.int32)[None, :, None]
    in_index = jnp.arange(outputs + taps - 1, dtype=jnp.int32)[None, None, :]
    offsets = jnp.arange(taps, dtype=jnp.int32)[:, None, None]
    return (in_index - out_index == offsets).astype(jnp.bfloat16)


def compare_pair(entries, first_place, second_place):
    larger = jnp.maximum(entries[first_place], entries[second_place])
    smaller = jnp.minimum(entries[first_place], entries[second_place])
    entries[first_place] = larger
    entries[second_place] = smaller


def leading_four(values):
    grouped = values.reshape((values.shape[0] // 4, 4) + values.shape[1:])
    entries = [grouped[:, position] for position in range(4)]
    for first_place, second_place in ((0, 1), (2, 3), (0, 2), (1, 3), (1, 2)):
        compare_pair(entries, first_place, second_place)
    while entries[0].shape[0] > 1:
        if entries[0].shape[0] % 2:
            entries = [
                jnp.concatenate(
                    [member, jnp.full((1,) + member.shape[1:], -SENTINEL, member.dtype)], 0
                )
                for member in entries
            ]
        middle = entries[0].shape[0] // 2
        merged = [
            jnp.maximum(entries[position][:middle], entries[3 - position][middle:])
            for position in range(4)
        ]
        for first_place, second_place in ((0, 2), (1, 3), (0, 1), (2, 3)):
            compare_pair(merged, first_place, second_place)
        entries = merged
    return jnp.concatenate(entries, 0)


def usable_mask(slot_list, first_row, row_count, row_range, bad_bands, exposures_total):
    lookup = jnp.minimum(slot_list, exposures_total - 1)
    picker = (lookup[:, None] == jnp.arange(exposures_total, dtype=jnp.int32)[None, :]).astype(
        jnp.float32
    )
    bounds = jnp.dot(picker, row_range.astype(jnp.float32), precision=HIGHEST)
    flagged = jnp.dot(picker, bad_bands.astype(jnp.float32), precision=HIGHEST)
    row_place = (first_row + jnp.arange(row_count, dtype=jnp.int32)).astype(jnp.float32)
    row_fine = (
        (row_place[None, :] >= bounds[:, 0:1])
        & (row_place[None, :] < bounds[:, 1:2])
        & (slot_list < exposures_total)[:, None]
    )
    column_fine = jnp.repeat(flagged < 0.5, BAND_COLS, axis=1)
    return row_fine[:, :, None] & column_fine[:, None, :]


def usable_count(first_row, row_count, row_range, bad_bands):
    row_place = (first_row + jnp.arange(row_count, dtype=jnp.int32)).astype(jnp.float32)
    bounds = row_range.astype(jnp.float32)
    covered = (
        (row_place[None, :] >= bounds[:, 0:1]) & (row_place[None, :] < bounds[:, 1:2])
    ).astype(jnp.float32)
    clean = (bad_bands == 0).astype(jnp.float32)
    per_band = jnp.dot(covered.T, clean, precision=HIGHEST)
    return jnp.repeat(per_band, BAND_COLS, axis=1).astype(jnp.int32)


def finish_pixels(grand_total, top_sum, bottom_sum, cover_count, exposures_total):
    clipped = cover_count >= MIN_VALID
    used_count = jnp.where(clipped, cover_count - 2 * REJECT, cover_count)
    kept_sum = jnp.where(clipped, grand_total - top_sum - bottom_sum, grand_total)
    coadd_plane = kept_sum / jnp.maximum(used_count, 1).astype(jnp.float32)
    return (coadd_plane, exposures_total - used_count)


def general_shards(
    exposures, slot_ids, row_range, bad_bands, kernel_choice, flux_scale, vert_taps, horiz_taps
):
    slot_count, row_dev, columns = exposures.shape
    exposures_total = flux_scale.shape[0]
    kernels = vert_taps.shape[0]
    margin = TAPS // 2
    band_count = columns // BAND_COLS
    expo_size = lax.axis_size("expo")
    expo_place = lax.axis_index("expo")
    sky_place = lax.axis_index("sky")
    negative_fill = jnp.asarray(-SENTINEL, jnp.bfloat16)
    own_slots = lax.dynamic_index_in_dim(slot_ids, expo_place, 0, keepdims=False)
    own_lookup = jnp.minimum(own_slots, exposures_total - 1)
    picker = (own_lookup[:, None] == jnp.arange(exposures_total, dtype=jnp.int32)[None, :]).astype(
        jnp.float32
    )
    chosen = jnp.dot(picker, kernel_choice.astype(jnp.float32), precision=HIGHEST)
    selector = (chosen[:, :, None] == jnp.arange(kernels, dtype=jnp.float32)[None, None, :]).astype(
        jnp.bfloat16
    )
    factor = jnp.dot(picker, flux_scale, precision=HIGHEST)
    block_rows = min(row_dev, 128)
    vertical_bank = jnp.einsum(
        "kt,tij->kij", vert_taps, shift_table(block_rows, TAPS), preferred_element_type=jnp.float32
    ).astype(jnp.bfloat16)
    vertical_pick = jnp.einsum(
        "sbk,kij->sbij", selector, vertical_bank, preferred_element_type=jnp.float32
    ).astype(jnp.bfloat16)
    widened = padded_2(exposures, (("sky", 1),), margin)
    widened = widened.reshape(slot_count, row_dev + 2 * margin, band_count, BAND_COLS)
    vertical_blocks = jnp.einsum(
        "sbij,sjbc->sibc", vertical_pick, widened, preferred_element_type=jnp.float32
    )
    vertical = vertical_blocks.astype(jnp.bfloat16).reshape(slot_count, row_dev, columns)
    horizontal_bank = jnp.einsum(
        "kt,tcj->kjc", horiz_taps, shift_table(BAND_COLS, TAPS), preferred_element_type=jnp.float32
    ).astype(jnp.bfloat16)
    horizontal_pick = jnp.einsum(
        "sbk,kjc->sbjc", selector, horizontal_bank, preferred_element_type=jnp.float32
    ).astype(jnp.bfloat16)
    padded = jnp.pad(vertical, ((0, 0), (0, 0), (margin, margin)))
    strips = jnp.stack(
        [
            padded[:, :, band_number * BAND_COLS : band_number * BAND_COLS + BAND_COLS + 2 * margin]
            for band_number in range(band_count)
        ],
        2,
    )
    filtered = jnp.einsum(
        "srbj,sbjc->srbc", strips, horizontal_pick, preferred_element_type=jnp.float32
    )
    planes = (filtered.reshape(slot_count, row_dev, columns) * factor[:, None, None]).astype(
        jnp.bfloat16
    )
    rows_out = row_dev // expo_size
    first_row = sky_place * row_dev + expo_place * rows_out
    cover_count = usable_count(first_row, rows_out, row_range, bad_bands)
    own_usable = usable_mask(
        own_slots, sky_place * row_dev, row_dev, row_range, bad_bands, exposures_total
    )
    partial_total = jnp.sum(
        jnp.where(own_usable, planes, jnp.zeros((), jnp.bfloat16)), axis=0, dtype=jnp.float32
    )[None]
    own_high = leading_four(jnp.where(own_usable, planes, negative_fill).reshape(slot_count, -1))
    own_low = leading_four(jnp.where(own_usable, -planes, negative_fill).reshape(slot_count, -1))
    extremes = jnp.concatenate([own_high, own_low], 0).reshape(8, row_dev, columns)
    received = lax.all_to_all(partial_total, "expo", split_axis=1, concat_axis=0, tiled=True)
    grand_total = jnp.sum(received, axis=0)
    arrived = lax.all_to_all(extremes, "expo", split_axis=1, concat_axis=0, tiled=True)
    senders = arrived.shape[0] // 8
    out_rows = arrived.shape[1]
    out_cols = arrived.shape[2]
    grouped = arrived.reshape(senders, 8, out_rows * out_cols)
    best_high = leading_four(grouped[:, :4].reshape(senders * 4, out_rows * out_cols))
    best_low = leading_four(grouped[:, 4:].reshape(senders * 4, out_rows * out_cols))
    high_sum = jnp.sum(best_high.astype(jnp.float32), axis=0).reshape(out_rows, out_cols)
    low_sum = -jnp.sum(best_low.astype(jnp.float32), axis=0).reshape(out_rows, out_cols)
    coadd_plane, rejected_count = finish_pixels(
        grand_total, high_sum, low_sum, cover_count, exposures_total
    )
    return (coadd_plane[None], rejected_count[None])


LANES = 128
FILL = 2.0**100
HALO = 16
UNROLL = 8
SORT_FOUR = ((0, 1), (2, 3), (0, 2), (1, 3), (1, 2))
SORT_BITONIC = ((0, 2), (1, 3), (0, 1), (2, 3))


def exchange(entries, places, first, second):
    for a, b in places:
        entries[a], entries[b] = first(entries[a], entries[b]), second(entries[a], entries[b])
    return entries


def merge_four(left, right, first, second, ordered=True):
    merged = [first(left[i], right[3 - i]) for i in range(4)]
    if ordered:
        exchange(merged, SORT_BITONIC, first, second)
    return merged


def flip_bit(place, bit):
    weight = 1 << bit
    return place + weight * (1 - 2 * ((place // weight) % 2))


def bit_order(band, steps):
    order = list(range(steps))
    return order


def flip_mask(place, mask, order):
    for position, bit in enumerate(order):
        if mask >> position & 1:
            place = flip_bit(place, bit)
    return place


def low_bit(mask, steps):
    for position in range(steps):
        if mask >> position & 1:
            return position
    return steps


def multiples(level, steps):
    masks = range(0, 1 << steps, 1 << level)
    return sorted(masks, key=lambda mask: -int(format(mask, f"0{steps}b")[::-1], 2))


def fused_kernel(
    senders,
    slot_ids,
    row_range,
    bad_bands,
    kernel_choice,
    flux_scale,
    range_table,
    band_table,
    vert_taps,
    horiz_taps,
    exposures,
    kept_out,
    used_out,
    pixels,
    taps,
    vertical_bank,
    horizontal_bank,
    columns_done,
    planes,
    extremes,
    totals,
    got_extremes,
    got_totals,
    load_sem,
    halo_send,
    halo_recv,
    ext_send,
    ext_recv,
    tot_send,
    tot_recv,
):
    slots, row_dev, columns = exposures.shape
    exposures_total = flux_scale.shape[0]
    kernels = vertical_bank.shape[0]
    bands = columns // BAND_COLS
    margin = TAPS // 2
    rows_out = row_dev // senders
    steps = senders.bit_length() - 1
    place = lax.axis_index("expo")
    sky = lax.axis_index("sky")

    for slot in range(slots):
        pltpu.make_async_copy(
            exposures.at[slot], pixels.at[slot, pl.ds(0, row_dev)], load_sem.at[slot]
        ).start()

    barrier = pltpu.get_barrier_semaphore()
    pl.semaphore_signal(barrier, 1, device_id={"sky": 1 - sky})
    for bit in range(steps):
        pl.semaphore_signal(barrier, 1, device_id={"expo": flip_bit(place, bit)})
    pl.semaphore_wait(barrier, steps + 1)

    edge = pl.multiple_of((1 - sky) * (row_dev - HALO), HALO)
    halo = pltpu.make_async_remote_copy(
        src_ref=exposures.at[:, pl.ds(edge, HALO)],
        dst_ref=pixels.at[:, pl.ds(row_dev, HALO)],
        send_sem=halo_send,
        recv_sem=halo_recv,
        device_id={"sky": 1 - sky},
    )
    halo.start()

    near = (
        jnp.abs(
            lax.broadcasted_iota(jnp.int32, (LANES, LANES), 0)
            - lax.broadcasted_iota(jnp.int32, (LANES, LANES), 1)
        )
        <= margin
    )

    taps[...] = jnp.zeros_like(taps)
    taps[0, 0:kernels, 0:TAPS] = vert_taps[...].astype(jnp.float32)
    taps[1, 0:kernels, 0:TAPS] = horiz_taps[...].astype(jnp.float32)
    for side in range(2):
        taps[side] = pltpu.roll(taps[side], LANES - margin % 8, 1)

    @pl.loop(0, kernels)
    def _(k):
        def circulant(side):
            spread = jnp.broadcast_to(taps[side, pl.ds(k, 1), :], (LANES, LANES))
            return pltpu.roll(spread, LANES - margin + margin % 8, 1, stride=1, stride_axis=0)

        vertical = circulant(0)
        outer = jnp.where(near, 0.0, vertical)
        outer = jnp.where(sky == 0, outer, pltpu.roll(outer, HALO, 1))
        vertical_bank[k, :, 0:LANES] = jnp.where(near, vertical, 0.0).astype(jnp.bfloat16)
        vertical_bank[k, :, LANES : LANES + HALO] = outer[:, :HALO].astype(jnp.bfloat16)
        horizontal = circulant(1).T
        horizontal_bank[k, 0:LANES, :] = jnp.where(near, horizontal, 0.0).astype(jnp.bfloat16)
        horizontal_bank[k, LANES : 2 * LANES, :] = jnp.where(near, 0.0, horizontal).astype(
            jnp.bfloat16
        )

    row_place = lax.broadcasted_iota(jnp.int32, (row_dev, LANES), 0) + sky * row_dev
    from_right = lax.broadcasted_iota(jnp.int32, (row_dev, LANES), 1) < LANES // 2

    halo.wait_recv()
    for slot in range(slots):
        pltpu.make_async_copy(
            exposures.at[slot], pixels.at[slot, pl.ds(0, row_dev)], load_sem.at[slot]
        ).wait()

    def entry_of(slot):
        return jnp.minimum(slot_ids[place, slot], exposures_total - 1)

    def filter_rows(slot, band):
        done = jnp.dot(
            vertical_bank[kernel_choice[band, entry_of(slot)]],
            pixels[slot, :, band * LANES : (band + 1) * LANES],
            preferred_element_type=jnp.float32,
        ).astype(jnp.bfloat16)
        columns_done[band, slot] = done
        return done

    def filter_band(band):
        @pl.loop(0, slots // UNROLL)
        def _(group):
            members = [group * UNROLL + i for i in range(UNROLL)]
            if band == 0:
                middle = [filter_rows(slot, 0) for slot in members]
            else:
                middle = [columns_done[band, slot] for slot in members]
            if band + 1 < bands:
                right = [filter_rows(slot, band + 1) for slot in members]
            for i, slot in enumerate(members):
                side = jnp.zeros((row_dev, LANES), jnp.float32)
                left = columns_done[band - 1, slot].astype(jnp.float32) if band else side
                side = right[i].astype(jnp.float32) if band + 1 < bands else side
                outer = jnp.where(from_right, side, left).astype(jnp.bfloat16)
                number = slot_ids[place, slot]
                entry = entry_of(slot)
                filtered = jnp.dot(
                    jnp.concatenate([middle[i], outer], axis=1),
                    horizontal_bank[kernel_choice[band, entry]],
                    preferred_element_type=jnp.float32,
                )
                open_band = (number < exposures_total) & (bad_bands[band, entry] == 0)
                last_row = jnp.where(open_band, row_range[1, entry], 0)
                usable = (row_place >= row_range[0, entry]) & (row_place < last_row)
                shown = jnp.where(usable, filtered * flux_scale[entry], -FILL)
                planes[slot] = shown.astype(jnp.bfloat16).reshape(senders, rows_out, LANES)

    def reduce_block(band, block):
        empty = jnp.asarray(-FILL, jnp.bfloat16)
        high = low = None
        total = jnp.zeros((rows_out, LANES), jnp.float32)
        for group in range(slots // 4):
            upper = [planes[4 * group + i, block] for i in range(4)]
            lower = []
            for i in range(4):
                gone = upper[i] == empty
                lower.append(jnp.where(gone, -empty, upper[i]))
                total += jnp.where(gone, jnp.zeros((), jnp.bfloat16), upper[i]).astype(jnp.float32)
            exchange(upper, SORT_FOUR, jnp.maximum, jnp.minimum)
            exchange(lower, SORT_FOUR, jnp.minimum, jnp.maximum)
            high = merge_four(high, upper, jnp.maximum, jnp.minimum) if group else upper
            low = merge_four(low, lower, jnp.minimum, jnp.maximum) if group else lower
        for i in range(4):
            extremes[band, block, i] = high[i]
            extremes[band, block, 4 + i] = low[i]
        totals[band, block] = total

    slot_of = {}
    for bit in range(steps):
        for mask in range(0, senders, 2 << bit):
            slot_of[bit, mask] = len(slot_of)

    def copies(band, mask):
        order = bit_order(band, steps)
        level = low_bit(mask, steps)
        block = flip_mask(place, mask, order)
        landing = slot_of[level, mask ^ (1 << level)]
        target = {"expo": flip_bit(place, order[level])}
        return (
            pltpu.make_async_remote_copy(
                src_ref=extremes.at[band, block],
                dst_ref=got_extremes.at[band, landing],
                send_sem=ext_send.at[band, landing],
                recv_sem=ext_recv.at[band, landing],
                device_id=target,
            ),
            pltpu.make_async_remote_copy(
                src_ref=totals.at[band, block],
                dst_ref=got_totals.at[band, landing],
                send_sem=tot_send.at[band, landing],
                recv_sem=tot_recv.at[band, landing],
                device_id=target,
            ),
        )

    started = []

    def send(band, mask):
        for copy in copies(band, mask):
            copy.start()
            started.append(copy)

    def start_band(band):
        filter_band(band)
        for mask in multiples(0, steps):
            reduce_block(band, flip_mask(place, mask, bit_order(band, steps)))
            if mask % 2:
                send(band, mask)

    def forward(band, level):
        for mask in multiples(level, steps):
            for copy in copies(band, mask ^ (1 << (level - 1))):
                copy.wait_recv()
            landing = slot_of[level - 1, mask]
            block = flip_mask(place, mask, bit_order(band, steps))
            mine = [extremes[band, block, i] for i in range(8)]
            theirs = [got_extremes[band, landing, i] for i in range(8)]
            ordered = level < steps
            high = merge_four(mine[:4], theirs[:4], jnp.maximum, jnp.minimum, ordered)
            low = merge_four(mine[4:], theirs[4:], jnp.minimum, jnp.maximum, ordered)
            total = totals[band, block] + got_totals[band, landing]
            if level == steps:
                finish(band, high, low, total)
                continue
            for i in range(4):
                extremes[band, block, i] = high[i]
                extremes[band, block, 4 + i] = low[i]
            totals[band, block] = total
            if low_bit(mask, steps) == level:
                send(band, mask)

    first_out = sky * row_dev + place * rows_out

    def finish(band, high, low, total):
        cols = slice(band * LANES, (band + 1) * LANES)
        out_place = lax.broadcasted_iota(jnp.int32, (rows_out, exposures_total), 0) + first_out
        covered = (out_place >= range_table[0:1, :]) & (out_place < range_table[1:2, :])
        clean = jnp.where(band_table[band : band + 1, :] == 0, 1.0, 0.0)
        count = lax.dot_general(
            jnp.where(covered, 1.0, 0.0).astype(jnp.bfloat16),
            jnp.broadcast_to(clean, (LANES, exposures_total)).astype(jnp.bfloat16),
            (((1,), (1,)), ((), ())),
            preferred_element_type=jnp.float32,
        )
        outer = sum(entry.astype(jnp.float32) for entry in high) + sum(
            entry.astype(jnp.float32) for entry in low
        )
        clipped = count >= MIN_VALID
        used = jnp.where(clipped, count - 2 * REJECT, count)
        kept_out[0, :, cols] = jnp.where(clipped, total - outer, total) / jnp.maximum(used, 1.0)
        used_out[0, :, cols] = (exposures_total - used).astype(jnp.int32)

    for turn in range(bands + steps):
        if turn < bands:
            start_band(turn)
        for level in range(1, steps + 1):
            if 0 <= turn - level < bands:
                forward(turn - level, level)

    halo.wait_send()
    for copy in started:
        copy.wait_send()


def relay_kernel(kept, used, kept_out, used_out):
    kept_out[...] = kept[...]
    used_out[...] = used[...]


def fused_shards(
    exposures, slot_ids, row_range, bad_bands, kernel_choice, flux_scale, vert_taps, horiz_taps
):
    slots, row_dev, columns = exposures.shape
    senders = lax.axis_size("expo")
    kernels = vert_taps.shape[0]
    rows_out = row_dev // senders
    smem = pl.BlockSpec(memory_space=pltpu.SMEM)
    vmem = pl.BlockSpec(memory_space=pltpu.VMEM)
    landings = senders - 1
    bands = columns // LANES
    kept, used = pl.pallas_call(
        functools.partial(fused_kernel, senders),
        out_shape=(
            jax.ShapeDtypeStruct((1, rows_out, columns), jnp.float32),
            jax.ShapeDtypeStruct((1, rows_out, columns), jnp.int32),
        ),
        in_specs=[smem] * 5 + [vmem] * 4 + [pl.BlockSpec(memory_space=pl.ANY)],
        out_specs=(vmem, vmem),
        scratch_shapes=[
            pltpu.VMEM((slots, row_dev + HALO, columns), jnp.bfloat16),
            pltpu.VMEM((2, -(-kernels // 8) * 8, LANES), jnp.float32),
            pltpu.VMEM((kernels, LANES, LANES + HALO), jnp.bfloat16),
            pltpu.VMEM((kernels, 2 * LANES, LANES), jnp.bfloat16),
            pltpu.VMEM((bands, slots, row_dev, LANES), jnp.bfloat16),
            pltpu.VMEM((slots, senders, rows_out, LANES), jnp.bfloat16),
            pltpu.VMEM((bands, senders, 8, rows_out, LANES), jnp.bfloat16),
            pltpu.VMEM((bands, senders, rows_out, LANES), jnp.float32),
            pltpu.VMEM((bands, landings, 8, rows_out, LANES), jnp.bfloat16),
            pltpu.VMEM((bands, landings, rows_out, LANES), jnp.float32),
            pltpu.SemaphoreType.DMA((slots,)),
            pltpu.SemaphoreType.DMA,
            pltpu.SemaphoreType.DMA,
            pltpu.SemaphoreType.DMA((bands, landings)),
            pltpu.SemaphoreType.DMA((bands, landings)),
            pltpu.SemaphoreType.DMA((bands, landings)),
            pltpu.SemaphoreType.DMA((bands, landings)),
        ],
        compiler_params=pltpu.CompilerParams(collective_id=0, has_side_effects=True),
    )(
        slot_ids,
        row_range.T,
        bad_bands.T,
        kernel_choice.T,
        flux_scale,
        row_range.T,
        bad_bands.T,
        vert_taps,
        horiz_taps,
        exposures,
    )
    return pl.pallas_call(
        relay_kernel,
        out_shape=(
            jax.ShapeDtypeStruct(kept.shape, kept.dtype),
            jax.ShapeDtypeStruct(used.shape, used.dtype),
        ),
        in_specs=[vmem] * 2,
        out_specs=(vmem, vmem),
    )(kept, used)


def shards(
    exposures, slot_ids, row_range, bad_bands, kernel_choice, flux_scale, vert_taps, horiz_taps
):
    slots, row_dev, columns = exposures.shape
    senders = lax.axis_size("expo")
    fits = (
        lax.axis_size("sky") == 2
        and senders & (senders - 1) == 0
        and senders > 1
        and row_dev == LANES
        and row_dev % (senders * 16) == 0
        and slots % max(4, UNROLL) == 0
        and columns % LANES == 0
    )
    chosen = fused_shards if fits else general_shards
    return chosen(
        exposures, slot_ids, row_range, bad_bands, kernel_choice, flux_scale, vert_taps, horiz_taps
    )


def solution(mesh):
    in_specs = (
        P(("groups", "expo"), "sky", None),
        P("groups", None),
        P("groups", None),
        P("groups", None),
        P("groups", None),
        P("groups"),
        P("groups", None),
        P("groups", None),
    )
    out_specs = (P(("groups", "sky"), "expo", None), P(("groups", "sky"), "expo", None))
    return jax.shard_map(shards, mesh=mesh, in_specs=in_specs, out_specs=out_specs, check_vma=False)
```

```python
import functools

import jax
import jax.numpy as jnp
from jax import lax
from jax.experimental import pallas as pl
from jax.experimental.pallas import tpu as pltpu
from jax.sharding import PartitionSpec as P

BAND_COLS = 128
TAPS = 21
REJECT = 4
MIN_VALID = 12


SENTINEL = 1e30
HIGHEST = lax.Precision.HIGHEST


def padded_2(cells, sides, width):
    for axis, dim in sides:
        count = lax.axis_size(axis)
        ends = count - 1
        head = lax.slice_in_dim(cells, 0, width, axis=dim)
        tail = lax.slice_in_dim(cells, cells.shape[dim] - width, cells.shape[dim], axis=dim)
        cells = jnp.concatenate(
            [
                lax.ppermute(tail, axis, [(i, (i + 1) % count) for i in range(ends)]),
                cells,
                lax.ppermute(head, axis, [((i + 1) % count, i) for i in range(ends)]),
            ],
            axis=dim,
        )
    return cells


def shift_table(outputs, taps):
    out_index = jnp.arange(outputs, dtype=jnp.int32)[None, :, None]
    in_index = jnp.arange(outputs + taps - 1, dtype=jnp.int32)[None, None, :]
    offsets = jnp.arange(taps, dtype=jnp.int32)[:, None, None]
    return (in_index - out_index == offsets).astype(jnp.bfloat16)


def compare_pair(entries, first_place, second_place):
    larger = jnp.maximum(entries[first_place], entries[second_place])
    smaller = jnp.minimum(entries[first_place], entries[second_place])
    entries[first_place] = larger
    entries[second_place] = smaller


def leading_four(values):
    grouped = values.reshape((values.shape[0] // 4, 4) + values.shape[1:])
    entries = [grouped[:, position] for position in range(4)]
    for first_place, second_place in ((0, 1), (2, 3), (0, 2), (1, 3), (1, 2)):
        compare_pair(entries, first_place, second_place)
    while entries[0].shape[0] > 1:
        if entries[0].shape[0] % 2:
            entries = [
                jnp.concatenate(
                    [member, jnp.full((1,) + member.shape[1:], -SENTINEL, member.dtype)], 0
                )
                for member in entries
            ]
        middle = entries[0].shape[0] // 2
        merged = [
            jnp.maximum(entries[position][:middle], entries[3 - position][middle:])
            for position in range(4)
        ]
        for first_place, second_place in ((0, 2), (1, 3), (0, 1), (2, 3)):
            compare_pair(merged, first_place, second_place)
        entries = merged
    return jnp.concatenate(entries, 0)


def usable_mask(slot_list, first_row, row_count, row_range, bad_bands, exposures_total):
    lookup = jnp.minimum(slot_list, exposures_total - 1)
    picker = (lookup[:, None] == jnp.arange(exposures_total, dtype=jnp.int32)[None, :]).astype(
        jnp.float32
    )
    bounds = jnp.dot(picker, row_range.astype(jnp.float32), precision=HIGHEST)
    flagged = jnp.dot(picker, bad_bands.astype(jnp.float32), precision=HIGHEST)
    row_place = (first_row + jnp.arange(row_count, dtype=jnp.int32)).astype(jnp.float32)
    row_fine = (
        (row_place[None, :] >= bounds[:, 0:1])
        & (row_place[None, :] < bounds[:, 1:2])
        & (slot_list < exposures_total)[:, None]
    )
    column_fine = jnp.repeat(flagged < 0.5, BAND_COLS, axis=1)
    return row_fine[:, :, None] & column_fine[:, None, :]


def usable_count(first_row, row_count, row_range, bad_bands):
    row_place = (first_row + jnp.arange(row_count, dtype=jnp.int32)).astype(jnp.float32)
    bounds = row_range.astype(jnp.float32)
    covered = (
        (row_place[None, :] >= bounds[:, 0:1]) & (row_place[None, :] < bounds[:, 1:2])
    ).astype(jnp.float32)
    clean = (bad_bands == 0).astype(jnp.float32)
    per_band = jnp.dot(covered.T, clean, precision=HIGHEST)
    return jnp.repeat(per_band, BAND_COLS, axis=1).astype(jnp.int32)


def finish_pixels(grand_total, top_sum, bottom_sum, cover_count, exposures_total):
    clipped = cover_count >= MIN_VALID
    used_count = jnp.where(clipped, cover_count - 2 * REJECT, cover_count)
    kept_sum = jnp.where(clipped, grand_total - top_sum - bottom_sum, grand_total)
    coadd_plane = kept_sum / jnp.maximum(used_count, 1).astype(jnp.float32)
    return (coadd_plane, exposures_total - used_count)


def general_shards(
    exposures, slot_ids, row_range, bad_bands, kernel_choice, flux_scale, vert_taps, horiz_taps
):
    slot_count, row_dev, columns = exposures.shape
    exposures_total = flux_scale.shape[0]
    kernels = vert_taps.shape[0]
    margin = TAPS // 2
    band_count = columns // BAND_COLS
    expo_size = lax.axis_size("expo")
    expo_place = lax.axis_index("expo")
    sky_place = lax.axis_index("sky")
    negative_fill = jnp.asarray(-SENTINEL, jnp.bfloat16)
    own_slots = lax.dynamic_index_in_dim(slot_ids, expo_place, 0, keepdims=False)
    own_lookup = jnp.minimum(own_slots, exposures_total - 1)
    picker = (own_lookup[:, None] == jnp.arange(exposures_total, dtype=jnp.int32)[None, :]).astype(
        jnp.float32
    )
    chosen = jnp.dot(picker, kernel_choice.astype(jnp.float32), precision=HIGHEST)
    selector = (chosen[:, :, None] == jnp.arange(kernels, dtype=jnp.float32)[None, None, :]).astype(
        jnp.bfloat16
    )
    factor = jnp.dot(picker, flux_scale, precision=HIGHEST)
    block_rows = min(row_dev, 128)
    vertical_bank = jnp.einsum(
        "kt,tij->kij", vert_taps, shift_table(block_rows, TAPS), preferred_element_type=jnp.float32
    ).astype(jnp.bfloat16)
    vertical_pick = jnp.einsum(
        "sbk,kij->sbij", selector, vertical_bank, preferred_element_type=jnp.float32
    ).astype(jnp.bfloat16)
    widened = padded_2(exposures, (("sky", 1),), margin)
    widened = widened.reshape(slot_count, row_dev + 2 * margin, band_count, BAND_COLS)
    vertical_blocks = jnp.einsum(
        "sbij,sjbc->sibc", vertical_pick, widened, preferred_element_type=jnp.float32
    )
    vertical = vertical_blocks.astype(jnp.bfloat16).reshape(slot_count, row_dev, columns)
    horizontal_bank = jnp.einsum(
        "kt,tcj->kjc", horiz_taps, shift_table(BAND_COLS, TAPS), preferred_element_type=jnp.float32
    ).astype(jnp.bfloat16)
    horizontal_pick = jnp.einsum(
        "sbk,kjc->sbjc", selector, horizontal_bank, preferred_element_type=jnp.float32
    ).astype(jnp.bfloat16)
    padded = jnp.pad(vertical, ((0, 0), (0, 0), (margin, margin)))
    strips = jnp.stack(
        [
            padded[:, :, band_number * BAND_COLS : band_number * BAND_COLS + BAND_COLS + 2 * margin]
            for band_number in range(band_count)
        ],
        2,
    )
    filtered = jnp.einsum(
        "srbj,sbjc->srbc", strips, horizontal_pick, preferred_element_type=jnp.float32
    )
    planes = (filtered.reshape(slot_count, row_dev, columns) * factor[:, None, None]).astype(
        jnp.bfloat16
    )
    rows_out = row_dev // expo_size
    first_row = sky_place * row_dev + expo_place * rows_out
    cover_count = usable_count(first_row, rows_out, row_range, bad_bands)
    own_usable = usable_mask(
        own_slots, sky_place * row_dev, row_dev, row_range, bad_bands, exposures_total
    )
    partial_total = jnp.sum(
        jnp.where(own_usable, planes, jnp.zeros((), jnp.bfloat16)), axis=0, dtype=jnp.float32
    )[None]
    own_high = leading_four(jnp.where(own_usable, planes, negative_fill).reshape(slot_count, -1))
    own_low = leading_four(jnp.where(own_usable, -planes, negative_fill).reshape(slot_count, -1))
    extremes = jnp.concatenate([own_high, own_low], 0).reshape(8, row_dev, columns)
    received = lax.all_to_all(partial_total, "expo", split_axis=1, concat_axis=0, tiled=True)
    grand_total = jnp.sum(received, axis=0)
    arrived = lax.all_to_all(extremes, "expo", split_axis=1, concat_axis=0, tiled=True)
    senders = arrived.shape[0] // 8
    out_rows = arrived.shape[1]
    out_cols = arrived.shape[2]
    grouped = arrived.reshape(senders, 8, out_rows * out_cols)
    best_high = leading_four(grouped[:, :4].reshape(senders * 4, out_rows * out_cols))
    best_low = leading_four(grouped[:, 4:].reshape(senders * 4, out_rows * out_cols))
    high_sum = jnp.sum(best_high.astype(jnp.float32), axis=0).reshape(out_rows, out_cols)
    low_sum = -jnp.sum(best_low.astype(jnp.float32), axis=0).reshape(out_rows, out_cols)
    coadd_plane, rejected_count = finish_pixels(
        grand_total, high_sum, low_sum, cover_count, exposures_total
    )
    return (coadd_plane[None], rejected_count[None])


LANES = 128
FILL = 2.0**100
HALO = 16
UNROLL = 12
SORT_FOUR = ((0, 1), (2, 3), (0, 2), (1, 3), (1, 2))
SORT_BITONIC = ((0, 2), (1, 3), (0, 1), (2, 3))


def exchange(entries, places, first, second):
    for a, b in places:
        entries[a], entries[b] = first(entries[a], entries[b]), second(entries[a], entries[b])
    return entries


def merge_four(left, right, first, second, ordered=True):
    merged = [first(left[i], right[3 - i]) for i in range(4)]
    if ordered:
        exchange(merged, SORT_BITONIC, first, second)
    return merged


def flip_bit(place, bit):
    weight = 1 << bit
    return place + weight * (1 - 2 * ((place // weight) % 2))


def bit_order(band, steps):
    order = list(range(steps))
    return order


def flip_mask(place, mask, order):
    for position, bit in enumerate(order):
        if mask >> position & 1:
            place = flip_bit(place, bit)
    return place


def low_bit(mask, steps):
    for position in range(steps):
        if mask >> position & 1:
            return position
    return steps


def multiples(level, steps):
    masks = range(0, 1 << steps, 1 << level)
    return sorted(masks, key=lambda mask: -int(format(mask, f"0{steps}b")[::-1], 2))


def fused_kernel(
    senders,
    slot_ids,
    row_range,
    bad_bands,
    kernel_choice,
    flux_scale,
    range_table,
    band_table,
    vert_taps,
    horiz_taps,
    exposures,
    kept_out,
    used_out,
    pixels,
    taps,
    vertical_bank,
    horizontal_bank,
    columns_done,
    planes,
    extremes,
    totals,
    got_extremes,
    got_totals,
    load_sem,
    halo_send,
    halo_recv,
    ext_send,
    ext_recv,
    tot_send,
    tot_recv,
):
    slots, row_dev, columns = exposures.shape
    exposures_total = flux_scale.shape[0]
    kernels = vertical_bank.shape[0]
    bands = columns // BAND_COLS
    margin = TAPS // 2
    rows_out = row_dev // senders
    steps = senders.bit_length() - 1
    place = lax.axis_index("expo")
    sky = lax.axis_index("sky")

    for slot in range(slots):
        pltpu.make_async_copy(
            exposures.at[slot], pixels.at[slot, pl.ds(0, row_dev)], load_sem.at[slot]
        ).start()

    barrier = pltpu.get_barrier_semaphore()
    pl.semaphore_signal(barrier, 1, device_id={"sky": 1 - sky})
    for bit in range(steps):
        pl.semaphore_signal(barrier, 1, device_id={"expo": flip_bit(place, bit)})
    pl.semaphore_wait(barrier, steps + 1)

    edge = pl.multiple_of((1 - sky) * (row_dev - HALO), HALO)
    halo = pltpu.make_async_remote_copy(
        src_ref=exposures.at[:, pl.ds(edge, HALO)],
        dst_ref=pixels.at[:, pl.ds(row_dev, HALO)],
        send_sem=halo_send,
        recv_sem=halo_recv,
        device_id={"sky": 1 - sky},
    )
    halo.start()

    near = (
        jnp.abs(
            lax.broadcasted_iota(jnp.int32, (LANES, LANES), 0)
            - lax.broadcasted_iota(jnp.int32, (LANES, LANES), 1)
        )
        <= margin
    )

    taps[...] = jnp.zeros_like(taps)
    taps[0, 0:kernels, 0:TAPS] = vert_taps[...].astype(jnp.float32)
    taps[1, 0:kernels, 0:TAPS] = horiz_taps[...].astype(jnp.float32)
    for side in range(2):
        taps[side] = pltpu.roll(taps[side], LANES - margin % 8, 1)

    @pl.loop(0, kernels)
    def _(k):
        def circulant(side):
            spread = jnp.broadcast_to(taps[side, pl.ds(k, 1), :], (LANES, LANES))
            return pltpu.roll(spread, LANES - margin + margin % 8, 1, stride=1, stride_axis=0)

        vertical = circulant(0)
        outer = jnp.where(near, 0.0, vertical)
        outer = jnp.where(sky == 0, outer, pltpu.roll(outer, HALO, 1))
        vertical_bank[k, :, 0:LANES] = jnp.where(near, vertical, 0.0).astype(jnp.bfloat16)
        vertical_bank[k, :, LANES : LANES + HALO] = outer[:, :HALO].astype(jnp.bfloat16)
        horizontal = circulant(1).T
        horizontal_bank[k, 0:LANES, :] = jnp.where(near, horizontal, 0.0).astype(jnp.bfloat16)
        horizontal_bank[k, LANES : 2 * LANES, :] = jnp.where(near, 0.0, horizontal).astype(
            jnp.bfloat16
        )

    row_place = lax.broadcasted_iota(jnp.int32, (row_dev, LANES), 0) + sky * row_dev
    from_right = lax.broadcasted_iota(jnp.int32, (row_dev, LANES), 1) < LANES // 2
    from_right = jnp.where(from_right, 1.0, 0.0).astype(jnp.bfloat16)

    halo.wait_recv()
    for slot in range(slots):
        pltpu.make_async_copy(
            exposures.at[slot], pixels.at[slot, pl.ds(0, row_dev)], load_sem.at[slot]
        ).wait()

    def entry_of(slot):
        return jnp.minimum(slot_ids[place, slot], exposures_total - 1)

    def filter_rows(slot, band):
        done = jnp.dot(
            vertical_bank[kernel_choice[band, entry_of(slot)]],
            pixels[slot, :, band * LANES : (band + 1) * LANES],
            preferred_element_type=jnp.float32,
        ).astype(jnp.bfloat16)
        columns_done[band, slot] = done
        return done

    def filter_band(band):
        @pl.loop(0, slots // UNROLL)
        def _(group):
            members = [group * UNROLL + i for i in range(UNROLL)]
            if band == 0:
                middle = [filter_rows(slot, 0) for slot in members]
            else:
                middle = [columns_done[band, slot] for slot in members]
            if band + 1 < bands:
                right = [filter_rows(slot, band + 1) for slot in members]
            for i, slot in enumerate(members):
                side = jnp.zeros((row_dev, LANES), jnp.bfloat16)
                left = columns_done[band - 1, slot] if band else side
                side = right[i] if band + 1 < bands else side
                outer = jnp.where(from_right > 0, side, left)
                number = slot_ids[place, slot]
                entry = entry_of(slot)
                filtered = jnp.dot(
                    jnp.concatenate([middle[i], outer], axis=1),
                    horizontal_bank[kernel_choice[band, entry]],
                    preferred_element_type=jnp.float32,
                )
                open_band = (number < exposures_total) & (bad_bands[band, entry] == 0)
                last_row = jnp.where(open_band, row_range[1, entry], 0)
                usable = (row_place >= row_range[0, entry]) & (row_place < last_row)
                shown = jnp.where(usable, filtered * flux_scale[entry], -FILL)
                planes[slot] = shown.astype(jnp.bfloat16).reshape(senders, rows_out, LANES)

    def reduce_block(band, block):
        empty = jnp.asarray(-FILL, jnp.bfloat16)
        high = low = None
        total = jnp.zeros((rows_out, LANES), jnp.float32)
        for group in range(slots // 4):
            upper = [planes[4 * group + i, block] for i in range(4)]
            lower = []
            for i in range(4):
                gone = upper[i] == empty
                lower.append(jnp.where(gone, -empty, upper[i]))
                total += jnp.where(gone, jnp.zeros((), jnp.bfloat16), upper[i]).astype(jnp.float32)
            exchange(upper, SORT_FOUR, jnp.maximum, jnp.minimum)
            exchange(lower, SORT_FOUR, jnp.minimum, jnp.maximum)
            high = merge_four(high, upper, jnp.maximum, jnp.minimum) if group else upper
            low = merge_four(low, lower, jnp.minimum, jnp.maximum) if group else lower
        for i in range(4):
            extremes[band, block, i] = high[i]
            extremes[band, block, 4 + i] = low[i]
        totals[band, block] = total

    slot_of = {}
    for bit in range(steps):
        for mask in range(0, senders, 2 << bit):
            slot_of[bit, mask] = len(slot_of)

    def copies(band, mask):
        order = bit_order(band, steps)
        level = low_bit(mask, steps)
        block = flip_mask(place, mask, order)
        landing = slot_of[level, mask ^ (1 << level)]
        target = {"expo": flip_bit(place, order[level])}
        return (
            pltpu.make_async_remote_copy(
                src_ref=extremes.at[band, block],
                dst_ref=got_extremes.at[band, landing],
                send_sem=ext_send.at[band, landing],
                recv_sem=ext_recv.at[band, landing],
                device_id=target,
            ),
            pltpu.make_async_remote_copy(
                src_ref=totals.at[band, block],
                dst_ref=got_totals.at[band, landing],
                send_sem=tot_send.at[band, landing],
                recv_sem=tot_recv.at[band, landing],
                device_id=target,
            ),
        )

    started = []

    def send(band, mask):
        for copy in copies(band, mask):
            copy.start()
            started.append(copy)

    def start_band(band):
        filter_band(band)
        for mask in multiples(0, steps):
            reduce_block(band, flip_mask(place, mask, bit_order(band, steps)))
            if mask % 2:
                send(band, mask)

    def forward(band, level):
        for mask in multiples(level, steps):
            for copy in copies(band, mask ^ (1 << (level - 1))):
                copy.wait_recv()
            landing = slot_of[level - 1, mask]
            block = flip_mask(place, mask, bit_order(band, steps))
            mine = [extremes[band, block, i] for i in range(8)]
            theirs = [got_extremes[band, landing, i] for i in range(8)]
            ordered = level < steps
            high = merge_four(mine[:4], theirs[:4], jnp.maximum, jnp.minimum, ordered)
            low = merge_four(mine[4:], theirs[4:], jnp.minimum, jnp.maximum, ordered)
            total = totals[band, block] + got_totals[band, landing]
            if level == steps:
                finish(band, high, low, total)
                continue
            for i in range(4):
                extremes[band, block, i] = high[i]
                extremes[band, block, 4 + i] = low[i]
            totals[band, block] = total
            if low_bit(mask, steps) == level:
                send(band, mask)

    first_out = sky * row_dev + place * rows_out

    def finish(band, high, low, total):
        cols = slice(band * LANES, (band + 1) * LANES)
        out_place = lax.broadcasted_iota(jnp.int32, (rows_out, exposures_total), 0) + first_out
        covered = (out_place >= range_table[0:1, :]) & (out_place < range_table[1:2, :])
        clean = jnp.where(band_table[band : band + 1, :] == 0, 1.0, 0.0)
        count = lax.dot_general(
            jnp.where(covered, 1.0, 0.0).astype(jnp.bfloat16),
            jnp.broadcast_to(clean, (LANES, exposures_total)).astype(jnp.bfloat16),
            (((1,), (1,)), ((), ())),
            preferred_element_type=jnp.float32,
        )
        outer = sum(entry.astype(jnp.float32) for entry in high) + sum(
            entry.astype(jnp.float32) for entry in low
        )
        clipped = count >= MIN_VALID
        used = jnp.where(clipped, count - 2 * REJECT, count)
        kept_out[0, :, cols] = jnp.where(clipped, total - outer, total) / jnp.maximum(used, 1.0)
        used_out[0, :, cols] = (exposures_total - used).astype(jnp.int32)

    for turn in range(bands + steps):
        if turn < bands:
            start_band(turn)
        for level in range(1, steps + 1):
            if 0 <= turn - level < bands:
                forward(turn - level, level)

    halo.wait_send()
    for copy in started:
        copy.wait_send()


def relay_kernel(kept, used, kept_out, used_out):
    kept_out[...] = kept[...]
    used_out[...] = used[...]


def fused_shards(
    exposures, slot_ids, row_range, bad_bands, kernel_choice, flux_scale, vert_taps, horiz_taps
):
    slots, row_dev, columns = exposures.shape
    senders = lax.axis_size("expo")
    kernels = vert_taps.shape[0]
    rows_out = row_dev // senders
    smem = pl.BlockSpec(memory_space=pltpu.SMEM)
    vmem = pl.BlockSpec(memory_space=pltpu.VMEM)
    landings = senders - 1
    bands = columns // LANES
    kept, used = pl.pallas_call(
        functools.partial(fused_kernel, senders),
        out_shape=(
            jax.ShapeDtypeStruct((1, rows_out, columns), jnp.float32),
            jax.ShapeDtypeStruct((1, rows_out, columns), jnp.int32),
        ),
        in_specs=[smem] * 5 + [vmem] * 4 + [pl.BlockSpec(memory_space=pl.ANY)],
        out_specs=(vmem, vmem),
        scratch_shapes=[
            pltpu.VMEM((slots, row_dev + HALO, columns), jnp.bfloat16),
            pltpu.VMEM((2, -(-kernels // 8) * 8, LANES), jnp.float32),
            pltpu.VMEM((kernels, LANES, LANES + HALO), jnp.bfloat16),
            pltpu.VMEM((kernels, 2 * LANES, LANES), jnp.bfloat16),
            pltpu.VMEM((bands, slots, row_dev, LANES), jnp.bfloat16),
            pltpu.VMEM((slots, senders, rows_out, LANES), jnp.bfloat16),
            pltpu.VMEM((bands, senders, 8, rows_out, LANES), jnp.bfloat16),
            pltpu.VMEM((bands, senders, rows_out, LANES), jnp.float32),
            pltpu.VMEM((bands, landings, 8, rows_out, LANES), jnp.bfloat16),
            pltpu.VMEM((bands, landings, rows_out, LANES), jnp.float32),
            pltpu.SemaphoreType.DMA((slots,)),
            pltpu.SemaphoreType.DMA,
            pltpu.SemaphoreType.DMA,
            pltpu.SemaphoreType.DMA((bands, landings)),
            pltpu.SemaphoreType.DMA((bands, landings)),
            pltpu.SemaphoreType.DMA((bands, landings)),
            pltpu.SemaphoreType.DMA((bands, landings)),
        ],
        compiler_params=pltpu.CompilerParams(collective_id=0, has_side_effects=True),
    )(
        slot_ids,
        row_range.T,
        bad_bands.T,
        kernel_choice.T,
        flux_scale,
        row_range.T,
        bad_bands.T,
        vert_taps,
        horiz_taps,
        exposures,
    )
    return pl.pallas_call(
        relay_kernel,
        out_shape=(
            jax.ShapeDtypeStruct(kept.shape, kept.dtype),
            jax.ShapeDtypeStruct(used.shape, used.dtype),
        ),
        in_specs=[vmem] * 2,
        out_specs=(vmem, vmem),
    )(kept, used)


def shards(
    exposures, slot_ids, row_range, bad_bands, kernel_choice, flux_scale, vert_taps, horiz_taps
):
    slots, row_dev, columns = exposures.shape
    senders = lax.axis_size("expo")
    fits = (
        lax.axis_size("sky") == 2
        and senders & (senders - 1) == 0
        and senders > 1
        and row_dev == LANES
        and row_dev % (senders * 16) == 0
        and slots % max(4, UNROLL) == 0
        and columns % LANES == 0
    )
    chosen = fused_shards if fits else general_shards
    return chosen(
        exposures, slot_ids, row_range, bad_bands, kernel_choice, flux_scale, vert_taps, horiz_taps
    )


def solution(mesh):
    in_specs = (
        P(("groups", "expo"), "sky", None),
        P("groups", None),
        P("groups", None),
        P("groups", None),
        P("groups", None),
        P("groups"),
        P("groups", None),
        P("groups", None),
    )
    out_specs = (P(("groups", "sky"), "expo", None), P(("groups", "sky"), "expo", None))
    return jax.shard_map(shards, mesh=mesh, in_specs=in_specs, out_specs=out_specs, check_vma=False)
```
